128 devices in a mesh: grp: 4 (over x), tile: 32 (over z, y, core).
Axes of the slice: x: 4, y: 4, z: 4, core: 2. Of those that a mesh axis runs over, the one named last changes fastest.
Arguments:
- rhs_fiber: float32 [8192, 256], P(('grp', 'tile')), may hold values from -6 to 6
- rhs_body: float32 [400, 4608], P('grp', 'tile'), may hold values from -6 to 6
- fiber_ops: bfloat16 [8192, 256, 256], P(('grp', 'tile')), may hold values from -0.375 to 0.375
- body_op: bfloat16 [4608, 4608], P('tile'), may hold values from -0.09375 to 0.09375
- positions: float32 [3, 524288], P(None, ('grp', 'tile')), may hold values from 0 to 1
- send_order: int32 [128, 4096], P(('grp', 'tile')), may hold values from 0 to 4095, each once within a row
- leaf_order: int32 [128, 4096], P(('grp', 'tile')), may hold values from 0 to 4095, each once within a row
- neighbours: int32 [4096, 2], P(('grp', 'tile')), may hold values 0 or 1
- attach_nucleus: int32 [8192], P(('grp', 'tile')), may hold values from 0 to 99
- attach_node: int32 [8192], P(('grp', 'tile')), may hold values from 0 to 1535
Outputs:
- sol_fiber: float32 [8192, 256], P(('grp', 'tile'))
- sol_body: float32 [400, 4608], P('grp', 'tile')
The draws below stay inside these ranges and needn't reach their ends.
Inputs may be any that keep to these rules, and one draw needn't show every extreme that they name: `send_order`: each row is a permutation of the device's 4096 node positions, so each device sends exactly 4096 / 32 nodes to every device of its group. `leaf_order`: each row is a permutation of the device's 4096 received slots.
All inputs are finite; a program needn't handle non-finite values. No bound on the sum of `neighbours` on one device may be relied on, other than what follows from the above.
Results may differ from the reference program's by a relative error of at most 0.002.
Values may be sent and summed in bfloat16 or wider, within the bound.
No kernel may reach another device: no remote copies, remote signals or barrier semaphores. Data moves between devices by JAX's collectives and lax.ppermute only.
A program may use at most 128 MiB of HBM per device.

```python
import math
import jax
import jax.numpy as jnp
from jax import lax

FNODES = 64
BNODES = 1536
FIB_DEV = 64
NUC_GRP = 100
LEAF_PTS = 128
ITERS = 3
ORDER = 256
BCOLS = 4608
NODE_DEV = 4096
FIBERS = 8192
NODES = 524288
NUCLEI = 400
LEAVES = 4096
N_GRP = 4
N_TILE = 32


def plant(entries, key, low, high):
    dims = entries.shape
    index_at = [jax.random.randint(jax.random.fold_in(key, axis), (), 0, dims[axis]) for axis in range(len(dims))]
    entries = entries.at[tuple(index_at)].set(low)
    longest = dims.index(max(dims))
    index_at[longest] = (index_at[longest] + 1) % dims[longest]
    return entries.at[tuple(index_at)].set(high)


def block_scale(key, shape, cuts, low, top_value):
    def one(axis_at, blocks):
        heights = jax.random.uniform(jax.random.fold_in(jax.random.fold_in(key, 6), axis_at), (blocks,), jnp.float32, low / len(cuts), top_value / len(cuts))
        return jnp.repeat(jnp.exp(heights), shape[axis_at] // blocks).reshape((-1,) + (1,) * (len(shape) - axis_at - 1))

    factor_of = one(*cuts[0])
    for cut in cuts[1:]:
        factor_of = factor_of * one(*cut)
    return factor_of


def normal_values(own_key, shape, deviation, bound, shards=(), kind=jnp.bfloat16):
    loudness = block_scale(own_key, shape, shards, -0.22, 0.18) if shards else 1.0
    values = jax.random.normal(own_key, shape, jnp.float32) * deviation * loudness
    return jnp.minimum(jnp.maximum(values, -bound), bound).astype(kind)


def setup_inputs(seed: int = 0) -> dict:
    arg_keys = jax.random.split(jax.random.key(seed), 11)
    rhs_fiber = normal_values(arg_keys[0], (FIBERS, ORDER), 1.0, 6.0, ((0, 128),), jnp.float32)
    rhs_body = normal_values(arg_keys[1], (NUCLEI, BCOLS), 1.0, 6.0, ((0, 4), (1, 32)), jnp.float32)
    fiber_ops = normal_values(arg_keys[2], (FIBERS, ORDER, ORDER), ORDER ** -0.5, 0.375, ((0, 128),))
    body_op = normal_values(arg_keys[3], (BCOLS, BCOLS), BCOLS ** -0.5, 0.09375, ((0, 32),))
    positions = jnp.clip(1.0 * jax.random.uniform(arg_keys[4], (3, NODES), jnp.float32) ** block_scale(arg_keys[4], (3, NODES), ((1, 128),), -0.2, 0.2), 0.0, 1.0)
    send_order = jax.vmap(lambda own: jax.random.permutation(own, NODE_DEV))(jax.random.split(arg_keys[5], (N_GRP * N_TILE))).reshape((N_GRP * N_TILE, NODE_DEV)).astype(jnp.int32)
    leaf_order = jax.vmap(lambda own: jax.random.permutation(own, NODE_DEV))(jax.random.split(arg_keys[6], (N_GRP * N_TILE))).reshape((N_GRP * N_TILE, NODE_DEV)).astype(jnp.int32)
    neighbours = plant((jax.random.randint(arg_keys[7], (LEAVES, 2), 0, 4) < 3).astype(jnp.int32), jax.random.fold_in(arg_keys[7], 1), 0, 1)
    attach_nucleus = plant(jax.random.randint(arg_keys[8], (FIBERS,), 0, NUC_GRP), jax.random.fold_in(arg_keys[8], 1), 0, NUC_GRP - 1).astype(jnp.int32)
    attach_node = plant(jax.random.randint(arg_keys[9], (FIBERS,), 0, BNODES), jax.random.fold_in(arg_keys[9], 1), 0, BNODES - 1).astype(jnp.int32)
    return dict(rhs_fiber=rhs_fiber, rhs_body=rhs_body, fiber_ops=fiber_ops, body_op=body_op, positions=positions, send_order=send_order, leaf_order=leaf_order, neighbours=neighbours, attach_nucleus=attach_nucleus, attach_node=attach_node)


kappa_coef = 0.5
eps_square = 0.0025
stokes_coef = 1.0 / (16.0 * math.pi)

def stokes_block(target_pos, source_pos, source_force):
    delta_pos = target_pos[:, :, :, None] - source_pos[:, :, None, :]
    dist_square = lax.optimization_barrier(jnp.sum(delta_pos * delta_pos, axis=1))
    along_force = lax.optimization_barrier(jnp.sum(delta_pos * source_force[:, :, None, :], axis=1))
    inv_root = lax.rsqrt(dist_square + eps_square)
    inv_cube = inv_root * inv_root * inv_root
    terms = (source_force[:, :, None, :] * (dist_square + 2.0 * eps_square)[:, None] + delta_pos * along_force[:, None]) * inv_cube[:, None]
    return stokes_coef * lax.optimization_barrier(jnp.sum(terms, axis=3))

def window_velocity(leaf_pos, pos_left, pos_right, leaf_force, force_left, force_right, leaf_masks, block_size):
    source_pos = jnp.concatenate([pos_left, leaf_pos, pos_right], axis=2)
    source_force = jnp.concatenate([force_left * leaf_masks[:, 0, None, None], leaf_force, force_right * leaf_masks[:, 1, None, None]], axis=2)
    leaf_count = leaf_pos.shape[0]

    def shaped(array):
        return array.reshape((leaf_count // block_size, block_size) + array.shape[1:])

    def one_block(pieces):
        return stokes_block(pieces[0], pieces[1], pieces[2])
    result = lax.map(one_block, (shaped(leaf_pos), shaped(source_pos), shaped(source_force)))
    return result.reshape(leaf_pos.shape)

def unpermute(values, order_rows):

    def one_device(value_block, order_block):
        return jnp.zeros_like(value_block).at[:, order_block].set(value_block)
    return jax.vmap(one_device, in_axes=(1, 0), out_axes=1)(values, order_rows)

def group_shift(leaf_array, direction):
    shaped = leaf_array.reshape((N_GRP, -1) + leaf_array.shape[1:])
    zero_leaf = jnp.zeros_like(shaped[:, :1])
    if direction < 0:
        moved = jnp.concatenate([zero_leaf, shaped[:, :-1]], axis=1)
    else:
        moved = jnp.concatenate([shaped[:, 1:], zero_leaf], axis=1)
    return moved.reshape(leaf_array.shape)

def route_to_leaves(node_values, send_order, leaf_order):
    all_devices = N_GRP * N_TILE
    share = NODE_DEV // N_TILE
    shaped = node_values.reshape(3, all_devices, NODE_DEV)
    sent = jnp.take_along_axis(shaped, send_order[None], axis=2)
    received = sent.reshape(3, N_GRP, N_TILE, N_TILE, share).transpose(0, 1, 3, 2, 4).reshape(3, all_devices, NODE_DEV)
    in_leaves = jnp.take_along_axis(received, leaf_order[None], axis=2)
    return in_leaves.reshape(3, LEAVES, LEAF_PTS).transpose(1, 0, 2)

def route_back(leaf_values, send_order, leaf_order):
    all_devices = N_GRP * N_TILE
    share = NODE_DEV // N_TILE
    flat = leaf_values.transpose(1, 0, 2).reshape(3, all_devices, NODE_DEV)
    in_slots = unpermute(flat, leaf_order)
    returned = in_slots.reshape(3, N_GRP, N_TILE, N_TILE, share).transpose(0, 1, 3, 2, 4).reshape(3, all_devices, NODE_DEV)
    return unpermute(returned, send_order).reshape(3, NODES)

def apply_operator(fiber_vec, nucleus_vec, fiber_ops, body_op, leaf_pos, send_order, leaf_order, leaf_masks, nucleus_rows, nucleus_cols):
    all_devices = N_GRP * N_TILE
    fiber_bf = fiber_vec.astype(jnp.bfloat16)
    nucleus_bf = nucleus_vec.astype(jnp.bfloat16)

    def per_device(pieces):
        return jnp.einsum('fij,fj->fi', pieces[0].astype(jnp.float32), pieces[1].astype(jnp.float32))
    fiber_prod = lax.map(per_device, (fiber_ops.reshape(all_devices, FIB_DEV, ORDER, ORDER), fiber_bf.reshape(all_devices, FIB_DEV, ORDER)))
    fiber_out = fiber_vec + fiber_prod.reshape(FIBERS, ORDER)
    nucleus_out = nucleus_vec + jnp.dot(nucleus_bf.astype(jnp.float32), body_op.T.astype(jnp.float32), preferred_element_type=jnp.float32)
    end_cols = jnp.arange(3) * FNODES
    fiber_out = fiber_out.at[:, end_cols].add(-kappa_coef * nucleus_bf[nucleus_rows[:, None], nucleus_cols].astype(jnp.float32))
    nucleus_out = nucleus_out.at[nucleus_rows[:, None], nucleus_cols].add(-kappa_coef * fiber_vec[:, end_cols])
    forces = fiber_vec[:, :3 * FNODES].reshape(FIBERS, 3, FNODES).transpose(1, 0, 2).reshape(3, NODES)
    leaf_force = route_to_leaves(forces, send_order, leaf_order)
    block_size = math.gcd(LEAVES, 64)
    velocity = window_velocity(leaf_pos, group_shift(leaf_pos, -1), group_shift(leaf_pos, 1), leaf_force, group_shift(leaf_force, -1), group_shift(leaf_force, 1), leaf_masks, block_size)
    node_vel = route_back(velocity, send_order, leaf_order)
    hydro_term = node_vel.reshape(3, FIBERS, FNODES).transpose(1, 0, 2).reshape(FIBERS, 3 * FNODES)
    fiber_out = fiber_out + jnp.concatenate([hydro_term, jnp.zeros((FIBERS, FNODES), jnp.float32)], axis=1)
    return (fiber_out, nucleus_out)

def inner_product(first, second):
    return jnp.sum(first[0] * second[0]) + jnp.sum(first[1] * second[1])

def reference(rhs_fiber, rhs_body, fiber_ops, body_op, positions, send_order, leaf_order, neighbours, attach_nucleus, attach_node):
    leaf_pos = route_to_leaves(positions, send_order, leaf_order)
    leaf_masks = neighbours.astype(jnp.float32)
    fiber_group = jnp.arange(FIBERS, dtype=jnp.int32) // (FIB_DEV * N_TILE)
    nucleus_rows = fiber_group * NUC_GRP + attach_nucleus
    nucleus_cols = (jnp.arange(3, dtype=jnp.int32) * BNODES)[None, :] + attach_node[:, None]
    start_norm = jnp.sqrt(inner_product((rhs_fiber, rhs_body), (rhs_fiber, rhs_body)))
    basis = [(rhs_fiber / start_norm, rhs_body / start_norm)]
    hessen = jnp.zeros((ITERS + 1, ITERS), jnp.float32)
    for j in range(ITERS):
        image = apply_operator(basis[j][0], basis[j][1], fiber_ops, body_op, leaf_pos, send_order, leaf_order, leaf_masks, nucleus_rows, nucleus_cols)
        coeffs = [inner_product(image, vector) for vector in basis]
        fiber_w, nucleus_w = image
        for i in range(j + 1):
            fiber_w = fiber_w - coeffs[i] * basis[i][0]
            nucleus_w = nucleus_w - coeffs[i] * basis[i][1]
        new_length = jnp.sqrt(inner_product((fiber_w, nucleus_w), (fiber_w, nucleus_w)))
        for i in range(j + 1):
            hessen = hessen.at[i, j].set(coeffs[i])
        hessen = hessen.at[j + 1, j].set(new_length)
        if j + 1 < ITERS:
            basis.append((fiber_w / new_length, nucleus_w / new_length))
    gram = jnp.dot(hessen.T, hessen, precision=lax.Precision.HIGHEST)
    target = start_norm * hessen[0, :]
    factor = jnp.linalg.cholesky(gram)
    weights = jax.scipy.linalg.cho_solve((factor, True), target)
    sol_fiber = jnp.zeros_like(rhs_fiber)
    sol_body = jnp.zeros_like(rhs_body)
    for j in range(ITERS):
        sol_fiber = sol_fiber + weights[j] * basis[j][0]
        sol_body = sol_body + weights[j] * basis[j][1]
    return (sol_fiber, sol_body)
```

```python
import functools
import math

import jax
import jax.numpy as jnp
from jax import lax
from jax.experimental import pallas as pl
from jax.experimental.pallas import tpu as pltpu
from jax.sharding import PartitionSpec as P

FNODES = 64
BNODES = 1536
ITERS = 3
FIB = 64
NUC = 100
ORDER = 256
COLS = 144
ROWS = 32
LANES = 128
NODES = ROWS * LANES
PAYLOAD = 152
TILES = 32
ALL = 128

kappa_coef = 0.5
eps_square = 0.0025
stokes_coef = 1.0 / (16.0 * math.pi)

F32 = jnp.float32
BF16 = jnp.bfloat16
AXES = ("grp", "tile")


def shape(dims, dtype=F32):
    return jax.ShapeDtypeStruct(dims, dtype)


VMEM = pl.BlockSpec(memory_space=pltpu.VMEM)
SMEM = pl.BlockSpec(memory_space=pltpu.SMEM)


def call(body, outs, in_specs, scratch=(), micros=1.0):
    return pl.pallas_call(
        body,
        out_shape=outs,
        in_specs=in_specs,
        out_specs=jax.tree.map(lambda _: VMEM, outs),
        scratch_shapes=list(scratch),
        cost_estimate=pl.CostEstimate(
            flops=0, transcendentals=0, bytes_accessed=int(micros * 3.6e6)
        ),
    )


def lane_iota(rows):
    return lax.broadcasted_iota(jnp.int32, (rows, LANES), 1)


def sub_iota(rows):
    return lax.broadcasted_iota(jnp.int32, (rows, LANES), 0)


def pick(read, count, row, lane):
    outs = [jnp.zeros((ROWS, LANES), F32)] * count
    for r in range(ROWS):
        hit = row == r
        for c in range(count):
            source = jnp.broadcast_to(read(c, r), (ROWS, LANES))
            found = jnp.take_along_axis(source, lane, axis=1, mode="promise_in_bounds")
            outs[c] = jnp.where(hit, found, outs[c])
    return outs


def swap_out(mix, parts, out_ref, width):
    for c in range(width):
        mix[c * ROWS : (c + 1) * ROWS, :] = parts[min(c, len(parts) - 1)]
    for d in range(ROWS):
        out_ref[d] = mix[pl.ds(d, width, stride=ROWS), :]


def fiber_table(q_ref):
    low = lane_iota(ROWS) < FNODES
    a0, a1 = q_ref[:ROWS, :LANES], q_ref[:ROWS, LANES:]
    b0, b1 = q_ref[ROWS:, :LANES], q_ref[ROWS:, LANES:]
    t0 = jnp.where(low, a0, pltpu.roll(b0, FNODES, 1))
    t1 = jnp.where(low, pltpu.roll(a0, FNODES, 1), b0)
    t2 = jnp.where(low, a1, pltpu.roll(b1, FNODES, 1))
    return t0, t1, t2


def table_place(node):
    row = (node >> 6) & 31
    lane = ((node >> 11) << 6) | (node & 63)
    return row, lane


def prep_kernel(pos_ref, q_ref, order_ref, att_ref, sent_ref, index_ref, table, mix):
    for r in range(ROWS):
        index_ref[r : r + 1, :] = order_ref[:, r * LANES : (r + 1) * LANES]
    node = index_ref[...]
    spots = pick(
        lambda c, r: pos_ref[c : c + 1, r * LANES : (r + 1) * LANES], 3, node >> 7, node & 127
    )
    for c, part in enumerate(fiber_table(q_ref)):
        table[c] = part
    row, lane = table_place(node)
    forces = pick(lambda c, r: table[c, r : r + 1, :], 3, row, lane)
    extra = [jnp.broadcast_to(att_ref[i : i + 1, :], (ROWS, LANES)) for i in range(2)]
    swap_out(mix, spots + forces + extra, sent_ref, 8)


def invert_kernel(leaf_ref, send_ref, index_ref, inv_leaf_ref, inv_send_ref):
    slots = lane_iota(64)
    upper = sub_iota(64) >= 32
    spot = sub_iota(64) & 31

    def one(place, row_of, lane_of):
        value = slots + place * LANES
        digit = jnp.where(upper, value & 63, value >> 6).astype(F32)
        left = jnp.where(row_of == spot, digit, 0.0).astype(BF16)
        right = jnp.where(lane_of == sub_iota(LANES), 1.0, 0.0).astype(BF16)
        return lax.dot_general(
            left, right, (((1,), (1,)), ((), ())), preferred_element_type=F32
        )

    leaf_sum = jnp.zeros((64, LANES), F32)
    send_sum = jnp.zeros((64, LANES), F32)
    for r in range(ROWS):
        leaf = leaf_ref[:, r * LANES : (r + 1) * LANES]
        index_ref[r : r + 1, :] = leaf
        leaf_sum = leaf_sum + one(r, leaf >> 7, leaf & 127)
        row, lane = table_place(send_ref[:, r * LANES : (r + 1) * LANES])
        send_sum = send_sum + one(r, row, lane)
    for total, ref in ((leaf_sum, inv_leaf_ref), (send_sum, inv_send_ref)):
        ref[...] = (total[:32] * 64.0 + total[32:]).astype(jnp.int32)


def payload_kernel(q_ref, z_ref, out_ref):
    out_ref[:COLS, :] = z_ref[...].astype(BF16)
    rows = []
    for half in range(2):
        part = q_ref[:, half * LANES : (half + 1) * LANES]
        high = part.astype(BF16).astype(F32)
        rows.append(jnp.concatenate([high, part - high], axis=0).T)
    where = sub_iota(8)
    ends = jnp.where(
        where == 0,
        rows[0][0:1, :],
        jnp.where(where == 1, rows[0][FNODES : FNODES + 1, :], rows[1][0:1, :]),
    )
    out_ref[COLS:, :] = ends.astype(BF16)


def leaf_kernel(first, recv_ref, index_ref, *outs):
    slot = index_ref[...]
    base = 0
    if first:
        pos_ref, force_ref, head_ref, tail_ref = outs
        parts = pick(lambda c, r: recv_ref[r, c : c + 1, :], 6, slot >> 7, slot & 127)
        for c in range(3):
            pos_ref[c] = parts[c]
            head_ref[c : c + 1, :] = parts[c][:1]
            tail_ref[c : c + 1, :] = parts[c][ROWS - 1 :]
        base = 3
    else:
        force_ref, head_ref, tail_ref = outs
        parts = pick(lambda c, r: recv_ref[r, c : c + 1, :], 3, slot >> 7, slot & 127)
    for c in range(3):
        part = parts[base + c] * stokes_coef
        force_ref[c] = part
        head_ref[3 + c : 4 + c, :] = part[:1]
        tail_ref[3 + c : 4 + c, :] = part[ROWS - 1 :]
    for c in (6, 7) if first else (0, 1, 2, 6, 7):
        head_ref[c : c + 1, :] = jnp.zeros((1, LANES), F32)
        tail_ref[c : c + 1, :] = jnp.zeros((1, LANES), F32)


def pair_sum(target, sources, total):
    for spot, force in sources:
        dx, dy, dz = (target[c] - spot[c] for c in range(3))
        along = dx * force[0] + dy * force[1] + dz * force[2]
        square = dx * dx + dy * dy + dz * dz
        root = lax.rsqrt(square + eps_square)
        cube = root * root * root
        near = (square + 2.0 * eps_square) * cube
        along = along * cube
        total = [
            t + (near * f + along * d) for t, f, d in zip(total, force, (dx, dy, dz))
        ]
    return total


def leaf_sum(target_row, sources, column, total):
    for c in range(3):
        column[c] = jnp.broadcast_to(target_row(c), (LANES, LANES)).T
    spread = [
        tuple([jnp.broadcast_to(v, (8, LANES)) for v in part] for part in source)
        for source in sources
    ]
    for g in range(LANES // 8):
        rows = slice(g * 8, g * 8 + 8)
        start = [jnp.zeros((8, LANES), F32)] * 3
        found = pair_sum([column[c, rows, :] for c in range(3)], spread, start)
        for c in range(3):
            total[c, rows, :] = found[c]
    return [jnp.sum(total[c].T, axis=0, keepdims=True) for c in range(3)]


def stokes_kernel(mask_ref, pos_ref, force_ref, out_ref, column, total):
    def leaf(i, carry):
        def rows(ref, j):
            return [ref[c, pl.ds(j, 1), :] for c in range(3)]

        before, after = jnp.maximum(i - 1, 0), jnp.minimum(i + 1, ROWS - 1)
        weak = jnp.where(i > 0, mask_ref[i, 0], 0.0)
        strong = jnp.where(i < ROWS - 1, mask_ref[i, 1], 0.0)
        sources = [
            (rows(pos_ref, i), rows(force_ref, i)),
            (rows(pos_ref, before), [f * weak for f in rows(force_ref, before)]),
            (rows(pos_ref, after), [f * strong for f in rows(force_ref, after)]),
        ]
        found = leaf_sum(lambda c: pos_ref[c, pl.ds(i, 1), :], sources, column, total)
        for c in range(3):
            out_ref[c, pl.ds(i, 1), :] = found[c]
        return carry

    lax.fori_loop(0, ROWS, leaf, 0)


def halo_kernel(
    mask_ref, vel_ref, pos_ref, bpos_ref, apos_ref, bfor_ref, afor_ref, inv_ref, out_ref,
    column, total, field, mix,
):
    field[...] = vel_ref[...]
    for i, side, spot, force in ((0, 0, bpos_ref, bfor_ref), (ROWS - 1, 1, apos_ref, afor_ref)):
        source = (
            [spot[c : c + 1, :] for c in range(3)],
            [force[3 + c : 4 + c, :] * mask_ref[i, side] for c in range(3)],
        )
        found = leaf_sum(lambda c: pos_ref[c, i : i + 1, :], [source], column, total)
        for c in range(3):
            field[c, i : i + 1, :] = field[c, i : i + 1, :] + found[c]
    slot = inv_ref[...]
    parts = pick(lambda c, r: field[c, r : r + 1, :], 3, slot >> 7, slot & 127)
    swap_out(mix, parts, out_ref, 4)


def body_kernel(base_ref, got_ref, op_ref, take_ref, mine_ref, recv_ref, z_ref, corr_ref):
    full = got_ref[:, :COLS, :].reshape(TILES * COLS, LANES)
    z = jnp.dot(op_ref[...], full, preferred_element_type=F32)
    got = jnp.dot(take_ref[...], full, preferred_element_type=F32)
    mine = mine_ref[...]
    lane = lane_iota(FIB)
    corr = jnp.zeros((FIB, LANES), F32)
    for c in range(3):
        value = jnp.sum(got[c * FIB : (c + 1) * FIB] * mine, axis=1, keepdims=True)
        corr = jnp.where(lane == c, value * -kappa_coef, corr)
    corr_ref[...] = corr
    column = (sub_iota(COLS) + base_ref[0]).astype(F32)
    nucleus = sub_iota(LANES).astype(F32)
    ends = jnp.zeros((COLS, LANES), F32)
    for s in range(TILES):
        node = recv_ref[s, 7:8, :]
        left = jnp.zeros((COLS, LANES), F32)
        for c in range(3):
            value = got_ref[s, COLS + c : COLS + c + 1, :].astype(F32)
            left = jnp.where(column == node + float(c * BNODES), value, left)
        right = jnp.where(nucleus == recv_ref[s, 6:7, :], 1.0, 0.0).astype(BF16)
        ends = ends + lax.dot_general(
            left.astype(BF16), right, (((1,), (1,)), ((), ())), preferred_element_type=F32
        )
    z_ref[...] = z - kappa_coef * ends


def assemble(back_ref, inv_ref, prod_ref, corr_ref, q_ref):
    slot = inv_ref[...]
    h0, h1, h2 = pick(lambda c, r: back_ref[r, c : c + 1, :], 3, slot >> 7, slot & 127)
    lane = lane_iota(ROWS)
    low = lane < FNODES
    blank = jnp.zeros((ROWS, LANES), F32)
    first = (
        jnp.where(low, h0, pltpu.roll(h1, FNODES, 1)),
        jnp.where(low, pltpu.roll(h0, FNODES, 1), h1),
    )
    second = (jnp.where(low, h2, blank), jnp.where(low, pltpu.roll(h2, FNODES, 1), blank))
    for half in range(2):
        rows = slice(half * ROWS, (half + 1) * ROWS)
        c0, c1, c2 = (corr_ref[rows, c : c + 1] for c in range(3))
        at0 = jnp.where(lane == 0, c0, jnp.where(lane == FNODES, c1, blank))
        at1 = jnp.where(lane == 0, c2, blank)
        q_ref[rows, :LANES] = prod_ref[rows, :LANES] + first[half] + at0
        q_ref[rows, LANES:] = prod_ref[rows, LANES:] + second[half] + at1


def join_kernel(back_ref, inv_ref, prod_ref, corr_ref, index_ref, q_ref, sent_ref, table, mix):
    assemble(back_ref, inv_ref, prod_ref, corr_ref, q_ref)
    for c, part in enumerate(fiber_table(q_ref)):
        table[c] = part
    row, lane = table_place(index_ref[...])
    forces = pick(lambda c, r: table[c, r : r + 1, :], 3, row, lane)
    swap_out(mix, forces, sent_ref, 4)


def dots_kernel(back_ref, inv_ref, prod_ref, corr_ref, *refs):
    q, z, (out_ref, last) = refs[:3], refs[3:7], refs[7:]
    assemble(back_ref, inv_ref, prod_ref, corr_ref, last)
    q = list(q) + [last]
    lane = lane_iota(1)
    line = jnp.zeros((1, LANES), F32)
    k = 0
    for i in range(4):
        for j in range(i + 1):
            total = jnp.sum(q[i][...] * q[j][...]) + jnp.sum(z[i][...] * z[j][...])
            line = jnp.where(lane == k, total, line)
            k += 1
    for d in range(ALL):
        out_ref[d] = line


def solve_kernel(gram_ref, *refs):
    q, z, (fiber_ref, body_ref) = refs[:3], refs[3:6], refs[6:]
    line = jnp.sum(gram_ref[...], axis=0)
    lane = lane_iota(1)
    g = {}
    k = 0
    for i in range(4):
        for j in range(i + 1):
            g[i, j] = g[j, i] = jnp.sum(jnp.where(lane == k, line, 0.0), axis=1, keepdims=True)
            k += 1
    n = {}
    for i in range(3):
        for j in range(i + 1):
            n[i, j] = g[i, j] + g[i + 1, j] + g[i, j + 1] + g[i + 1, j + 1]
    t = [g[0, i] + g[0, i + 1] for i in range(3)]
    l00 = jnp.sqrt(n[0, 0])
    l10, l20 = n[1, 0] / l00, n[2, 0] / l00
    l11 = jnp.sqrt(n[1, 1] - l10 * l10)
    l21 = (n[2, 1] - l20 * l10) / l11
    l22 = jnp.sqrt(n[2, 2] - l20 * l20 - l21 * l21)
    f0 = t[0] / l00
    f1 = (t[1] - l10 * f0) / l11
    f2 = (t[2] - l20 * f0 - l21 * f1) / l22
    c2 = f2 / l22
    c1 = (f1 - l21 * c2) / l11
    c0 = (f0 - l10 * c1 - l20 * c2) / l00
    fiber_ref[...] = c0 * q[0][...] + c1 * q[1][...] + c2 * q[2][...]
    body_ref[...] = c0 * z[0][...] + c1 * z[1][...] + c2 * z[2][...]


def exchange(array, axis="tile"):
    return lax.all_to_all(array, axis, split_axis=0, concat_axis=0, tiled=True)


def local(
    rhs_fiber,
    rhs_body,
    fiber_ops,
    body_op,
    positions,
    send_order,
    leaf_order,
    neighbours,
    attach_nucleus,
    attach_node,
):
    base = (lax.axis_index("tile") * COLS).astype(jnp.int32).reshape(1)
    masks = neighbours.astype(F32)
    up = [(i, i + 1) for i in range(TILES - 1)]
    down = [(i + 1, i) for i in range(TILES - 1)]
    body0 = jnp.pad(rhs_body.T, ((0, 0), (0, LANES - NUC)))
    att = jnp.stack([jnp.tile(attach_nucleus, 2), jnp.tile(attach_node, 2)]).astype(F32)
    wanted = (jnp.arange(3, dtype=jnp.int32)[:, None] * BNODES + attach_node[None, :]).reshape(-1)
    take = (wanted[:, None] == jnp.arange(3 * BNODES, dtype=jnp.int32)[None, :]).astype(BF16)
    mine = (attach_nucleus[:, None] == jnp.arange(LANES, dtype=jnp.int32)[None, :]).astype(F32)

    square = shape((ROWS, LANES), jnp.int32)
    field = shape((3, ROWS, LANES))
    edge = shape((8, LANES))
    tile3 = pltpu.VMEM((3, LANES, LANES), F32)
    table = pltpu.VMEM((3, ROWS, LANES), F32)
    mix8 = pltpu.VMEM((8 * ROWS, LANES), F32)
    mix4 = pltpu.VMEM((4 * ROWS, LANES), F32)

    sent, send_index = call(
        prep_kernel, (shape((ROWS, 8, LANES)), square), [VMEM] * 4, [table, mix8], 2.0
    )(positions, rhs_fiber, send_order, att)
    leaf_index, inv_leaf, inv_send = call(
        invert_kernel, (square, square, square), [VMEM] * 2, (), 2.0
    )(leaf_order, send_order)

    q, z = [rhs_fiber], [body0]
    info = pos = before0 = after0 = None
    for j in range(ITERS):
        recv = exchange(sent)
        payload = call(payload_kernel, shape((PAYLOAD, LANES), BF16), [VMEM] * 2)(q[j], z[j])
        got = exchange(jnp.broadcast_to(payload[None], (TILES, PAYLOAD, LANES)))
        product = jnp.einsum(
            "fij,fj->fi", fiber_ops, q[j].astype(BF16), preferred_element_type=F32
        )
        if j == 0:
            info = recv
            pos, force, head, tail = call(
                functools.partial(leaf_kernel, True), (field, field, edge, edge), [VMEM] * 2
            )(recv, leaf_index)
        else:
            force, head, tail = call(
                functools.partial(leaf_kernel, False), (field, edge, edge), [VMEM] * 2
            )(recv, leaf_index)
        before = lax.ppermute(tail, "tile", up)
        after = lax.ppermute(head, "tile", down)
        if j == 0:
            before0, after0 = before, after
        vel = call(stokes_kernel, field, [SMEM, VMEM, VMEM], [tile3, tile3], 8.0)(
            masks, pos, force
        )
        out = call(
            halo_kernel,
            shape((ROWS, 4, LANES)),
            [SMEM] + [VMEM] * 7,
            [tile3, tile3, table, mix4],
            2.0,
        )(masks, vel, pos, before0, after0, before, after, inv_leaf)
        back = exchange(out)
        image, corr = call(
            body_kernel,
            (shape((COLS, LANES)), shape((FIB, LANES))),
            [SMEM] + [VMEM] * 5,
            (),
            3.0,
        )(base, got, body_op, take, mine, info)
        z.append(image)
        if j + 1 < ITERS:
            vector, sent = call(
                join_kernel,
                (shape((FIB, ORDER)), shape((ROWS, 4, LANES))),
                [VMEM] * 5,
                [table, mix4],
                2.0,
            )(back, inv_send, product, corr, send_index)
            q.append(vector)
    line = call(
        dots_kernel,
        shape((ALL, 1, LANES)),
        [VMEM] * 11,
        [pltpu.VMEM((FIB, ORDER), F32)],
        2.0,
    )(back, inv_send, product, corr, *q, *z)
    gram = exchange(line, AXES)
    sol_fiber, sol_body = call(
        solve_kernel, (shape((FIB, ORDER)), shape((COLS, LANES))), [VMEM] * 7
    )(gram, *q, *z[:3])
    return sol_fiber, sol_body[:, :NUC].T


def solution(mesh):
    placed = (
        P(AXES, None),
        P("grp", "tile"),
        P(AXES, None, None),
        P("tile", None),
        P(None, AXES),
        P(AXES, None),
        P(AXES, None),
        P(AXES, None),
        P(AXES),
        P(AXES),
    )
    return jax.shard_map(
        local,
        mesh=mesh,
        in_specs=placed,
        out_specs=(P(AXES, None), P("grp", "tile")),
        check_vma=False,
    )
```

```python
import functools
import math

import jax
import jax.numpy as jnp
from jax import lax
from jax.experimental import pallas as pl
from jax.experimental.pallas import tpu as pltpu
from jax.sharding import PartitionSpec as P

FNODES = 64
BNODES = 1536
ITERS = 3
FIB = 64
NUC = 100
ORDER = 256
COLS = 144
ROWS = 32
LANES = 128
NODES = ROWS * LANES
PITCH = 40
UNROLL = 4
TILES = 32
ALL = 128

kappa_coef = 0.5
eps_square = 0.0025
stokes_coef = 1.0 / (16.0 * math.pi)

F32 = jnp.float32
BF16 = jnp.bfloat16
TILE = ("chip", "core")
AXES = ("grp",) + TILE


def shape(dims, dtype=F32):
    return jax.ShapeDtypeStruct(dims, dtype)


VMEM = pl.BlockSpec(memory_space=pltpu.VMEM)
SMEM = pl.BlockSpec(memory_space=pltpu.SMEM)


def call(body, outs, in_specs, scratch=(), micros=1.0):
    return pl.pallas_call(
        body,
        out_shape=outs,
        in_specs=in_specs,
        out_specs=jax.tree.map(lambda _: VMEM, outs),
        scratch_shapes=list(scratch),
        cost_estimate=pl.CostEstimate(
            flops=0, transcendentals=0, bytes_accessed=int(micros * 3.6e6)
        ),
    )


def lane_iota(rows):
    return lax.broadcasted_iota(jnp.int32, (rows, LANES), 1)


def sub_iota(rows):
    return lax.broadcasted_iota(jnp.int32, (rows, LANES), 0)


def pick(read, count, row, lane):
    size = row.shape
    outs = [jnp.zeros(size, F32)] * count
    for r in range(ROWS):
        hit = row == r
        for c in range(count):
            source = jnp.broadcast_to(read(c, r), size)
            found = jnp.take_along_axis(source, lane, axis=1, mode="promise_in_bounds")
            outs[c] = jnp.where(hit, found, outs[c])
    return outs


def swap_out(mix, parts, out_ref, width):
    for c in range(width):
        mix[c * ROWS : (c + 1) * ROWS, :] = parts[min(c, len(parts) - 1)]
    for d in range(ROWS):
        out_ref[d] = mix[pl.ds(d, width, stride=ROWS), :]


def send_out(mix, parts, extras, out_ref, width):
    for c, part in enumerate(parts):
        mix[c * PITCH : c * PITCH + 1, :] = jnp.zeros((1, LANES), F32)
        mix[c * PITCH + ROWS + 1 : c * PITCH + ROWS + 2, :] = jnp.zeros((1, LANES), F32)
        mix[c * PITCH + 1 : c * PITCH + ROWS + 1, :] = part
    for b, rows in enumerate(extras):
        for k, row in enumerate(rows):
            c = len(parts) + k
            mix[c * PITCH : c * PITCH + PITCH, :] = jnp.broadcast_to(row, (PITCH, LANES))
        for d in range(ROWS):
            out_ref[d, b] = mix[pl.ds(d + b, width, stride=PITCH), :]


def end_rows(q_ref):
    turned = jnp.concatenate([q_ref[:, :LANES], q_ref[:, LANES:]], axis=0).T
    return turned[:1, :], turned[FNODES : FNODES + 1, :]


def fiber_table(q_ref):
    low = lane_iota(ROWS) < FNODES
    a0, a1 = q_ref[:ROWS, :LANES], q_ref[:ROWS, LANES:]
    b0, b1 = q_ref[ROWS:, :LANES], q_ref[ROWS:, LANES:]
    t0 = jnp.where(low, a0, pltpu.roll(b0, FNODES, 1))
    t1 = jnp.where(low, pltpu.roll(a0, FNODES, 1), b0)
    t2 = jnp.where(low, a1, pltpu.roll(b1, FNODES, 1))
    return t0, t1, t2


def table_place(node):
    row = (node >> 6) & 31
    lane = ((node >> 11) << 6) | (node & 63)
    return row, lane


def prep_kernel(
    pos_ref, q_ref, order_ref, leaf_ref, nuc_ref, node_ref, sent_ref, index_ref, table, mix
):
    for r in range(ROWS):
        index_ref[r : r + 1, :] = order_ref[:, r * LANES : (r + 1) * LANES]
    node = index_ref[...]
    spots = pick(
        lambda c, r: pos_ref[c : c + 1, r * LANES : (r + 1) * LANES], 3, node >> 7, node & 127
    )
    for c, part in enumerate(fiber_table(q_ref)):
        table[c] = part
    row, lane = table_place(node)
    forces = pick(lambda c, r: table[c, r : r + 1, :], 3, row, lane)
    twice = [jnp.concatenate([r[...], r[...]], axis=1).astype(F32) for r in (nuc_ref, node_ref)]
    rims = [leaf_ref[:, :LANES].astype(F32), leaf_ref[:, NODES - LANES :].astype(F32)]
    send_out(mix, spots + forces, [twice, list(end_rows(q_ref)), rims], sent_ref, 8)


def invert_kernel(
    leaf_ref, send_ref, body_ref, index_ref, inv_leaf_ref, inv_send_ref, z_ref, load_ref
):
    blank = jnp.zeros((COLS, LANES - NUC), F32)
    z = jnp.concatenate([body_ref[...], blank], axis=1)
    z_ref[...] = z
    for s in range(TILES // 2):
        load_ref[s] = z.astype(BF16)
    slots = lane_iota(64)
    upper = sub_iota(64) >= 32
    spot = sub_iota(64) & 31

    def one(place, row_of, lane_of):
        value = slots + place * LANES
        digit = jnp.where(upper, value & 63, value >> 6).astype(F32)
        left = jnp.where(row_of == spot, digit, 0.0).astype(BF16)
        right = jnp.where(lane_of == sub_iota(LANES), 1.0, 0.0).astype(BF16)
        return lax.dot_general(
            left, right, (((1,), (1,)), ((), ())), preferred_element_type=F32
        )

    leaf_sum = jnp.zeros((64, LANES), F32)
    send_sum = jnp.zeros((64, LANES), F32)
    for r in range(ROWS):
        leaf = leaf_ref[:, r * LANES : (r + 1) * LANES]
        index_ref[r : r + 1, :] = leaf
        leaf_sum = leaf_sum + one(r, leaf >> 7, leaf & 127)
        row, lane = table_place(send_ref[:, r * LANES : (r + 1) * LANES])
        send_sum = send_sum + one(r, row, lane)
    for total, ref in ((leaf_sum, inv_leaf_ref), (send_sum, inv_send_ref)):
        ref[...] = (total[:32] * 64.0 + total[32:]).astype(jnp.int32)


def pair_weights(target, spot, force):
    dx, dy, dz = (target[c] - spot[c] for c in range(3))
    root = lax.rsqrt((dx * dx + eps_square) + (dy * dy + dz * dz))
    cube = root * (root * root)
    along = (dx * force[0] + dy * force[1]) + dz * force[2]
    return root + eps_square * cube, along * cube


def halves(value):
    high = value.astype(BF16).astype(F32)
    return high, value - high


def near_kernel(first, tile_ref, mask_ref, recv_ref, index_ref, inv_ref, *refs):
    if first:
        out_ref, pos, rims_ref, force, lines, column, weight, total, mix = refs
        me = tile_ref[0]
        before, after = jnp.maximum(me - 1, 0), jnp.minimum(me + 1, TILES - 1)
        rims_ref[0:8, :] = jnp.broadcast_to(recv_ref[before, 2, 7:8, :], (8, LANES)).astype(
            jnp.int32
        )
        rims_ref[8:16, :] = jnp.broadcast_to(recv_ref[after, 2, 6:7, :], (8, LANES)).astype(
            jnp.int32
        )
        count, base = 6, 3
    else:
        pos, rims_ref, out_ref, force, lines, column, weight, total, mix = refs
        count, base = 3, 0
    slot = index_ref[...]
    parts = pick(lambda c, r: recv_ref[r, 1, c : c + 1, :], count, slot >> 7, slot & 127)
    ends = []
    for side in range(2):
        slot = rims_ref[8 * side : 8 * side + 8, :]
        block = 2 * side
        ends.append(
            pick(lambda c, r: recv_ref[r, block, c : c + 1, :], count, slot >> 7, slot & 127)
        )
    live = (
        jnp.where(tile_ref[0] > 0, stokes_coef, 0.0),
        jnp.where(tile_ref[0] < TILES - 1, stokes_coef, 0.0),
    )
    for c in range(3):
        if first:
            pos[c, 0:1, :] = ends[0][c][:1] - 0.5
            pos[c, 1 : ROWS + 1, :] = parts[c] - 0.5
            pos[c, ROWS + 1 : ROWS + 2, :] = ends[1][c][:1] - 0.5
            pos[c, ROWS + 2 :, :] = jnp.zeros((PITCH - ROWS - 2, LANES), F32)
        force[c, 0:1, :] = ends[0][base + c][:1] * live[0]
        force[c, 1 : ROWS + 1, :] = parts[base + c] * stokes_coef
        force[c, ROWS + 1 : ROWS + 2, :] = ends[1][base + c][:1] * live[1]
        force[c, ROWS + 2 :, :] = jnp.zeros((PITCH - ROWS - 2, LANES), F32)

    def plane(k):
        return slice(k * PITCH, (k + 1) * PITCH)

    lines[0, plane(6), :] = jnp.zeros((PITCH, LANES), F32)
    lines[0, plane(7), :] = jnp.zeros((PITCH, LANES), F32)
    lines[1, plane(6), :] = jnp.ones((PITCH, LANES), F32)
    lines[1, plane(7), :] = jnp.zeros((PITCH, LANES), F32)
    for k, ref in enumerate((force, pos)):
        for c in range(3):
            lines[k, plane(c), :], lines[k, plane(3 + c), :] = halves(ref[c])

    def one_leaf(i, u):
        for c in range(3):
            row = pos[c, pl.ds(i + 1, 1), :]
            column[u, c] = jnp.broadcast_to(row, (LANES, LANES)).T
        sums = [jnp.zeros((8, LANES), F32)] * 2
        for w in range(3):
            spot, push = (
                [jnp.broadcast_to(ref[c, pl.ds(i + w, 1), :], (8, LANES)) for c in range(3)]
                for ref in (pos, force)
            )
            for g in range(LANES // 16):
                found = [
                    pair_weights([column[u, c, h : h + 8, :] for c in range(3)], spot, push)
                    for h in (16 * g, 16 * g + 8)
                ]
                for k in range(2):
                    weight[u, k, w, 16 * g : 16 * g + 16, :] = jnp.concatenate(
                        [found[0][k], found[1][k]], axis=0
                    ).astype(BF16)
            for k in range(2):
                left = lines[k, pl.ds(i + w, 8, stride=PITCH), :].astype(BF16)
                part = lax.dot_general(
                    left, weight[u, k, w], (((1,), (1,)), ((), ())), preferred_element_type=F32
                )
                if w != 1:
                    part = part * mask_ref[i, w // 2].astype(F32)
                sums[k] = sums[k] + part
        for k in range(2):
            total[k, pl.ds(8 * i, 8), :] = sums[k]

    def leaves(i, carry):
        for u in range(UNROLL):
            one_leaf(i * UNROLL + u, u)
        return carry

    lax.fori_loop(0, ROWS // UNROLL, leaves, 0)

    def gathered(k, c):
        return total[k, pl.ds(c, ROWS, stride=8), :]

    weights = gathered(1, 6)
    for c in range(3):
        mix[c * ROWS : (c + 1) * ROWS, :] = (
            (gathered(0, c) + gathered(0, 3 + c))
            + pos[c, 1 : ROWS + 1, :] * weights
            - (gathered(1, c) + gathered(1, 3 + c))
        )
    slot = inv_ref[...]
    parts = pick(
        lambda c, r: mix[c * ROWS + r : c * ROWS + r + 1, :], 3, slot >> 7, slot & 127
    )
    swap_out(mix, parts, out_ref, 4)


def body_kernel(
    first, last, tile_ref, got_ref, mate_ref, op_ref, take_ref, mine_ref, info_ref, recv_ref,
    *refs,
):
    z_ref, corr_ref = refs[:2]
    rows, full_ref = refs[-2:]
    side = tile_ref[0] & 1
    for s in range(TILES // 2):
        full_ref[2 * s + side] = got_ref[s]
        full_ref[2 * s + 1 - side] = mate_ref[s]
    full = full_ref[...].reshape(TILES * COLS, LANES)
    z = jnp.dot(op_ref[...], full, preferred_element_type=F32)
    got = jnp.dot(take_ref[...], full, preferred_element_type=F32)
    mine = mine_ref[...]
    lane = lane_iota(FIB)
    corr = jnp.zeros((FIB, LANES), F32)
    for c in range(3):
        value = jnp.sum(got[c * FIB : (c + 1) * FIB] * mine, axis=1, keepdims=True)
        corr = jnp.where(lane == c, value * -kappa_coef, corr)
    corr_ref[...] = corr
    for s in range(TILES):
        rows[0, s : s + 1, :] = recv_ref[s, 1, 6:7, :] if first else recv_ref[s, 0, 3:4, :]
        rows[1, s : s + 1, :] = recv_ref[s, 1, 7:8, :] if first else recv_ref[s, 1, 3:4, :]
    low = lane_iota(TILES) < FNODES
    ra, rb = rows[0], rows[1]
    wa, wb = pltpu.roll(ra, FNODES, 1), pltpu.roll(rb, FNODES, 1)
    for c, value in enumerate(
        (jnp.where(low, ra, wa), jnp.where(low, rb, wb), jnp.where(low, wa, ra))
    ):
        high = value.astype(BF16).astype(F32)
        rows[c] = jnp.where(low, high, value - high)
    column = (sub_iota(COLS) + tile_ref[0] * COLS).astype(F32)
    nucleus = sub_iota(LANES).astype(F32)
    ends = jnp.zeros((COLS, LANES), F32)
    for s in range(TILES):
        node = info_ref[s, 0, 7:8, :]
        left = jnp.zeros((COLS, LANES), F32)
        for c in range(3):
            left = jnp.where(column == node + float(c * BNODES), rows[c, s : s + 1, :], left)
        right = jnp.where(nucleus == info_ref[s, 0, 6:7, :], 1.0, 0.0).astype(BF16)
        ends = ends + lax.dot_general(
            left.astype(BF16), right, (((1,), (1,)), ((), ())), preferred_element_type=F32
        )
    z = z - kappa_coef * ends
    z_ref[...] = z
    if not last:
        for s in range(TILES // 2):
            refs[2][s] = z.astype(BF16)


def assemble(back_ref, inv_ref, prod_ref, corr_ref, q_ref):
    slot = inv_ref[...]
    h0, h1, h2 = pick(lambda c, r: back_ref[r, c : c + 1, :], 3, slot >> 7, slot & 127)
    lane = lane_iota(ROWS)
    low = lane < FNODES
    blank = jnp.zeros((ROWS, LANES), F32)
    first = (
        jnp.where(low, h0, pltpu.roll(h1, FNODES, 1)),
        jnp.where(low, pltpu.roll(h0, FNODES, 1), h1),
    )
    second = (jnp.where(low, h2, blank), jnp.where(low, pltpu.roll(h2, FNODES, 1), blank))
    for half in range(2):
        rows = slice(half * ROWS, (half + 1) * ROWS)
        c0, c1, c2 = (corr_ref[rows, c : c + 1] for c in range(3))
        at0 = jnp.where(lane == 0, c0, jnp.where(lane == FNODES, c1, blank))
        at1 = jnp.where(lane == 0, c2, blank)
        q_ref[rows, :LANES] = prod_ref[rows, :LANES] + first[half] + at0
        q_ref[rows, LANES:] = prod_ref[rows, LANES:] + second[half] + at1


def join_kernel(
    back_ref, inv_ref, prod_ref, corr_ref, index_ref, q_ref, low_ref, sent_ref, table, mix
):
    assemble(back_ref, inv_ref, prod_ref, corr_ref, q_ref)
    low_ref[...] = q_ref[...].astype(BF16)
    for c, part in enumerate(fiber_table(q_ref)):
        table[c] = part
    row, lane = table_place(index_ref[...])
    forces = pick(lambda c, r: table[c, r : r + 1, :], 3, row, lane)
    even, odd = end_rows(q_ref)
    send_out(mix, forces, [[even], [odd], [odd]], sent_ref, 4)


def dots_kernel(back_ref, inv_ref, prod_ref, corr_ref, *refs):
    q, z, (out_ref, last) = refs[:3], refs[3:7], refs[7:]
    assemble(back_ref, inv_ref, prod_ref, corr_ref, last)
    q = list(q) + [last]
    lane = lane_iota(1)
    line = jnp.zeros((1, LANES), F32)
    k = 0
    for i in range(4):
        for j in range(i + 1):
            total = jnp.sum(q[i][...] * q[j][...]) + jnp.sum(z[i][...] * z[j][...])
            line = jnp.where(lane == k, total, line)
            k += 1
    for d in range(ALL):
        out_ref[d] = line


def solve_kernel(gram_ref, *refs):
    q, z, (fiber_ref, body_ref) = refs[:3], refs[3:6], refs[6:]
    line = jnp.sum(gram_ref[...], axis=0)
    lane = lane_iota(1)
    g = {}
    k = 0
    for i in range(4):
        for j in range(i + 1):
            g[i, j] = g[j, i] = jnp.sum(jnp.where(lane == k, line, 0.0), axis=1, keepdims=True)
            k += 1
    n = {}
    for i in range(3):
        for j in range(i + 1):
            n[i, j] = g[i, j] + g[i + 1, j] + g[i, j + 1] + g[i + 1, j + 1]
    t = [g[0, i] + g[0, i + 1] for i in range(3)]
    l00 = jnp.sqrt(n[0, 0])
    l10, l20 = n[1, 0] / l00, n[2, 0] / l00
    l11 = jnp.sqrt(n[1, 1] - l10 * l10)
    l21 = (n[2, 1] - l20 * l10) / l11
    l22 = jnp.sqrt(n[2, 2] - l20 * l20 - l21 * l21)
    f0 = t[0] / l00
    f1 = (t[1] - l10 * f0) / l11
    f2 = (t[2] - l20 * f0 - l21 * f1) / l22
    c2 = f2 / l22
    c1 = (f1 - l21 * c2) / l11
    c0 = (f0 - l10 * c1 - l20 * c2) / l00
    fiber_ref[...] = c0 * q[0][...] + c1 * q[1][...] + c2 * q[2][...]
    body = c0 * z[0][...] + c1 * z[1][...] + c2 * z[2][...]
    body_ref[...] = body[:, :NUC]


def exchange(array, axis=TILE):
    return lax.all_to_all(array, axis, split_axis=0, concat_axis=0, tiled=True)


def local(
    rhs_fiber,
    rhs_body,
    fiber_ops,
    body_op,
    positions,
    send_order,
    leaf_order,
    neighbours,
    attach_nucleus,
    attach_node,
):
    tile = lax.axis_index(TILE).astype(jnp.int32).reshape(1)
    load = shape((TILES // 2, COLS, LANES), BF16)
    wanted = (jnp.arange(3, dtype=jnp.int32)[:, None] * BNODES + attach_node[None, :]).reshape(-1)
    take = (wanted[:, None] == jnp.arange(3 * BNODES, dtype=jnp.int32)[None, :]).astype(BF16)
    mine = (attach_nucleus[:, None] == jnp.arange(LANES, dtype=jnp.int32)[None, :]).astype(F32)

    square = shape((ROWS, LANES), jnp.int32)
    spots = shape((3, PITCH, LANES))
    rims = shape((16, LANES), jnp.int32)
    table = pltpu.VMEM((3, ROWS, LANES), F32)
    padded = pltpu.VMEM((3, PITCH, LANES), F32)
    mix4 = pltpu.VMEM((4 * ROWS, LANES), F32)
    blocks8 = pltpu.VMEM((8 * PITCH, LANES), F32)
    blocks4 = pltpu.VMEM((4 * PITCH, LANES), F32)

    sent, send_index = call(
        prep_kernel, (shape((ROWS, 3, 8, LANES)), square), [VMEM] * 6, [table, blocks8], 2.0
    )(
        positions,
        rhs_fiber,
        send_order,
        leaf_order,
        attach_nucleus.reshape(1, FIB),
        attach_node.reshape(1, FIB),
    )
    leaf_index, inv_leaf, inv_send, body0, payload = call(
        invert_kernel,
        (square, square, square, shape((COLS, LANES)), load),
        [VMEM] * 3,
        (),
        2.0,
    )(leaf_order, send_order, rhs_body.T)

    q, z, low = [rhs_fiber], [body0], rhs_fiber.astype(BF16)
    for j in range(ITERS):
        first, last = j == 0, j + 1 == ITERS
        recv = exchange(sent)
        product = jnp.einsum(
            "fij,fj->fi", fiber_ops, low, preferred_element_type=F32
        )
        if first:
            recv, product, payload, take, mine = lax.optimization_barrier(
                (recv, product, payload, take, mine)
            )
        else:
            recv, product, payload = lax.optimization_barrier((recv, product, payload))
        got = exchange(payload, "chip")
        near = functools.partial(near_kernel, first)
        specs = [SMEM, SMEM] + [VMEM] * 3
        scratch = [
            padded,
            pltpu.VMEM((2, 8 * PITCH, LANES), F32),
            pltpu.VMEM((UNROLL, 3, LANES, LANES), F32),
            pltpu.VMEM((UNROLL, 2, 3, LANES, LANES), BF16),
            pltpu.VMEM((2, 8 * ROWS, LANES), F32),
            mix4,
        ]
        if first:
            info = recv
            out, pos, rim = call(
                near, (shape((ROWS, 4, LANES)), spots, rims), specs, scratch, 14.0
            )(tile, neighbours, recv, leaf_index, inv_leaf)
        else:
            out = call(near, shape((ROWS, 4, LANES)), specs + [VMEM] * 2, scratch, 14.0)(
                tile, neighbours, recv, leaf_index, inv_leaf, pos, rim
            )
        got, out = lax.optimization_barrier((got, out))
        mate = lax.ppermute(got, "core", [(0, 1), (1, 0)])
        back = exchange(out)
        made = [shape((COLS, LANES)), shape((FIB, LANES))]
        if not last:
            made.append(load)
        image, corr, *rest = call(
            functools.partial(body_kernel, first, last),
            tuple(made),
            [SMEM] + [VMEM] * 7,
            [pltpu.VMEM((3, TILES, LANES), F32), pltpu.VMEM((TILES, COLS, LANES), BF16)],
            4.0,
        )(tile, got, mate, body_op, take, mine, info, recv)
        z.append(image)
        if not last:
            payload = rest[0]
            vector, low, sent = call(
                join_kernel,
                (shape((FIB, ORDER)), shape((FIB, ORDER), BF16), shape((ROWS, 3, 4, LANES))),
                [VMEM] * 5,
                [table, blocks4],
                2.0,
            )(back, inv_send, product, corr, send_index)
            q.append(vector)
    line = call(
        dots_kernel,
        shape((ALL, 1, LANES)),
        [VMEM] * 11,
        [pltpu.VMEM((FIB, ORDER), F32)],
        2.0,
    )(back, inv_send, product, corr, *q, *z)
    gram = exchange(line, AXES)
    sol_fiber, sol_body = call(
        solve_kernel, (shape((FIB, ORDER)), shape((COLS, NUC))), [VMEM] * 7
    )(gram, *q, *z[:3])
    return sol_fiber, sol_body.T


def solution(mesh):
    groups, tiles = mesh.devices.shape
    split = jax.sharding.Mesh(mesh.devices.reshape(groups, tiles // 2, 2), AXES)
    placed = (
        P(AXES, None),
        P("grp", TILE),
        P(AXES, None, None),
        P(TILE, None),
        P(None, AXES),
        P(AXES, None),
        P(AXES, None),
        P(AXES, None),
        P(AXES),
        P(AXES),
    )
    return jax.shard_map(
        local,
        mesh=split,
        in_specs=placed,
        out_specs=(P(AXES, None), P("grp", TILE)),
        check_vma=False,
    )
```

```python
import functools
import math

import jax
import jax.numpy as jnp
from jax import lax
from jax.experimental import pallas as pl
from jax.experimental.pallas import tpu as pltpu
from jax.sharding import PartitionSpec as P

FNODES = 64
BNODES = 1536
ITERS = 3
FIB = 64
NUC = 100
ORDER = 256
COLS = 144
ROWS = 32
LANES = 128
NODES = ROWS * LANES
PITCH = 40
UNROLL = 4
BATCH = 8
TILES = 32
ALL = 128

kappa_coef = 0.5
eps_square = 0.0025
stokes_coef = 1.0 / (16.0 * math.pi)

F32 = jnp.float32
BF16 = jnp.bfloat16
TILE = ("chip", "core")
AXES = ("grp",) + TILE


def shape(dims, dtype=F32):
    return jax.ShapeDtypeStruct(dims, dtype)


VMEM = pl.BlockSpec(memory_space=pltpu.VMEM)
SMEM = pl.BlockSpec(memory_space=pltpu.SMEM)


def call(body, outs, in_specs, scratch=(), micros=1.0, grid=(), out_specs=None, mib=None):
    return pl.pallas_call(
        body,
        out_shape=outs,
        grid=grid,
        in_specs=in_specs,
        out_specs=out_specs or jax.tree.map(lambda _: VMEM, outs),
        scratch_shapes=list(scratch),
        compiler_params=pltpu.CompilerParams(vmem_limit_bytes=mib and mib << 20),
        cost_estimate=pl.CostEstimate(
            flops=0, transcendentals=0, bytes_accessed=int(micros * 3.6e6)
        ),
    )


def lane_iota(rows):
    return lax.broadcasted_iota(jnp.int32, (rows, LANES), 1)


def sub_iota(rows):
    return lax.broadcasted_iota(jnp.int32, (rows, LANES), 0)


def pick(read, count, row, lane):
    size = row.shape
    outs = [jnp.zeros(size, F32)] * count
    for r in range(ROWS):
        hit = row == r
        for c in range(count):
            source = jnp.broadcast_to(read(c, r), size)
            found = jnp.take_along_axis(source, lane, axis=1, mode="promise_in_bounds")
            outs[c] = jnp.where(hit, found, outs[c])
    return outs


def swap_out(mix, parts, out_ref, width):
    for c in range(width):
        mix[c * ROWS : (c + 1) * ROWS, :] = parts[min(c, len(parts) - 1)]
    for d in range(ROWS):
        out_ref[d] = mix[pl.ds(d, width, stride=ROWS), :]


def send_out(mix, parts, extras, out_ref, width):
    for c, part in enumerate(parts):
        mix[c * PITCH : c * PITCH + 1, :] = jnp.zeros((1, LANES), F32)
        mix[c * PITCH + ROWS + 1 : c * PITCH + ROWS + 2, :] = jnp.zeros((1, LANES), F32)
        mix[c * PITCH + 1 : c * PITCH + ROWS + 1, :] = part
    for b, rows in enumerate(extras):
        for k, row in enumerate(rows):
            c = len(parts) + k
            mix[c * PITCH : c * PITCH + PITCH, :] = jnp.broadcast_to(row, (PITCH, LANES))
        for d in range(ROWS):
            out_ref[d, b] = mix[pl.ds(d + b, width, stride=PITCH), :]


def end_rows(q_ref):
    turned = jnp.concatenate([q_ref[:, :LANES], q_ref[:, LANES:]], axis=0).T
    return turned[:1, :], turned[FNODES : FNODES + 1, :]


def fiber_table(q_ref):
    low = lane_iota(ROWS) < FNODES
    a0, a1 = q_ref[:ROWS, :LANES], q_ref[:ROWS, LANES:]
    b0, b1 = q_ref[ROWS:, :LANES], q_ref[ROWS:, LANES:]
    t0 = jnp.where(low, a0, pltpu.roll(b0, FNODES, 1))
    t1 = jnp.where(low, pltpu.roll(a0, FNODES, 1), b0)
    t2 = jnp.where(low, a1, pltpu.roll(b1, FNODES, 1))
    return t0, t1, t2


def table_place(node):
    row = (node >> 6) & 31
    lane = ((node >> 11) << 6) | (node & 63)
    return row, lane


def prep_kernel(
    pos_ref, q_ref, order_ref, leaf_ref, nuc_ref, node_ref, sent_ref, index_ref, table, mix
):
    for r in range(ROWS):
        index_ref[r : r + 1, :] = order_ref[:, r * LANES : (r + 1) * LANES]
    node = index_ref[...]
    spots = pick(
        lambda c, r: pos_ref[c : c + 1, r * LANES : (r + 1) * LANES], 3, node >> 7, node & 127
    )
    for c, part in enumerate(fiber_table(q_ref)):
        table[c] = part
    row, lane = table_place(node)
    forces = pick(lambda c, r: table[c, r : r + 1, :], 3, row, lane)
    twice = [jnp.concatenate([r[...], r[...]], axis=1).astype(F32) for r in (nuc_ref, node_ref)]
    rims = [leaf_ref[:, :LANES].astype(F32), leaf_ref[:, NODES - LANES :].astype(F32)]
    send_out(mix, spots + forces, [twice, list(end_rows(q_ref)), rims], sent_ref, 8)


def invert_kernel(
    leaf_ref, send_ref, body_ref, index_ref, inv_leaf_ref, inv_send_ref, z_ref, load_ref
):
    blank = jnp.zeros((COLS, LANES - NUC), F32)
    z = jnp.concatenate([body_ref[...], blank], axis=1)
    z_ref[...] = z
    for s in range(TILES // 2):
        load_ref[s] = z.astype(BF16)
    slots = lane_iota(64)
    upper = sub_iota(64) >= 32
    spot = sub_iota(64) & 31

    def one(place, row_of, lane_of):
        value = slots + place * LANES
        digit = jnp.where(upper, value & 63, value >> 6).astype(F32)
        left = jnp.where(row_of == spot, digit, 0.0).astype(BF16)
        right = jnp.where(lane_of == sub_iota(LANES), 1.0, 0.0).astype(BF16)
        return lax.dot_general(
            left, right, (((1,), (1,)), ((), ())), preferred_element_type=F32
        )

    leaf_sum = jnp.zeros((64, LANES), F32)
    send_sum = jnp.zeros((64, LANES), F32)
    for r in range(ROWS):
        leaf = leaf_ref[:, r * LANES : (r + 1) * LANES]
        index_ref[r : r + 1, :] = leaf
        leaf_sum = leaf_sum + one(r, leaf >> 7, leaf & 127)
        row, lane = table_place(send_ref[:, r * LANES : (r + 1) * LANES])
        send_sum = send_sum + one(r, row, lane)
    for total, ref in ((leaf_sum, inv_leaf_ref), (send_sum, inv_send_ref)):
        ref[...] = (total[:32] * 64.0 + total[32:]).astype(jnp.int32)


def pair_weights(target, spot, force):
    dx, dy, dz = (target[c] - spot[c] for c in range(3))
    root = lax.rsqrt((dx * dx + eps_square) + (dy * dy + dz * dz))
    cube = root * (root * root)
    along = (dx * force[0] + dy * force[1]) + dz * force[2]
    return root + eps_square * cube, cube, along * cube


def halves(value):
    high = value.astype(BF16).astype(F32)
    return high, value - high


def near_kernel(first, tile_ref, mask_ref, recv_ref, index_ref, inv_ref, *refs):
    if first:
        out_ref, pos, rims_ref, near_ref, cube_ref = refs[:5]
    else:
        pos, rims_ref, near_ref, cube_ref, out_ref = refs[:5]
    force, lines, column, weight, total, mix = refs[5:]
    step = pl.program_id(0)

    @pl.when(step == 0)
    def _():
        gather_leaves(
            first, tile_ref, recv_ref, index_ref, pos, rims_ref, force, lines
        )

    def one_leaf(b, u):
        i = step * BATCH + b
        for c in range(3):
            row = pos[c, pl.ds(i + 1, 1), :]
            column[u, c] = jnp.broadcast_to(row, (LANES, LANES)).T
        sums = [jnp.zeros((8, LANES), F32)] * 2
        for w in range(3):
            spot, push = (
                [jnp.broadcast_to(ref[c, pl.ds(i + w, 1), :], (8, LANES)) for c in range(3)]
                for ref in (pos, force)
            )
            inner = (spot[0] * push[0] + spot[1] * push[1]) + spot[2] * push[2]
            for g in range(LANES // 16):
                rows = slice(16 * g, 16 * g + 16)
                found = []
                for h in (16 * g, 16 * g + 8):
                    target = [column[u, c, h : h + 8, :] for c in range(3)]
                    if first:
                        near, cube, turn = pair_weights(target, spot, push)
                        cube_ref[b, w, h : h + 8, :] = cube
                        found.append((turn, near))
                    else:
                        along = (target[0] * push[0] + target[1] * push[1]) + (
                            target[2] * push[2] - inner
                        )
                        found.append((along * cube_ref[b, w, h : h + 8, :],))
                halves_of = [jnp.concatenate(k, axis=0).astype(BF16) for k in zip(*found)]
                weight[u, w, rows, :] = halves_of[0]
                if first:
                    near_ref[b, w, rows, :] = halves_of[1]
            for k, right in enumerate((near_ref[b, w], weight[u, w])):
                left = lines[k, pl.ds(i + w, 8, stride=PITCH), :].astype(BF16)
                part = lax.dot_general(
                    left, right, (((1,), (1,)), ((), ())), preferred_element_type=F32
                )
                if w != 1:
                    part = part * mask_ref[i, w // 2].astype(F32)
                sums[k] = sums[k] + part
        for k in range(2):
            total[k, pl.ds(8 * i, 8), :] = sums[k]

    def leaves(i, carry):
        for u in range(UNROLL):
            one_leaf(i * UNROLL + u, u)
        return carry

    lax.fori_loop(0, BATCH // UNROLL, leaves, 0)

    @pl.when(step == ROWS // BATCH - 1)
    def _():
        weights = total[1, pl.ds(6, ROWS, stride=8), :]

        def gathered(k, c):
            return total[k, pl.ds(c, ROWS, stride=8), :]

        for c in range(3):
            mix[c * ROWS : (c + 1) * ROWS, :] = (
                (gathered(0, c) + gathered(0, 3 + c))
                + pos[c, 1 : ROWS + 1, :] * weights
                - (gathered(1, c) + gathered(1, 3 + c))
            )
        slot = inv_ref[...]
        parts = pick(
            lambda c, r: mix[c * ROWS + r : c * ROWS + r + 1, :], 3, slot >> 7, slot & 127
        )
        swap_out(mix, parts, out_ref, 4)


def gather_leaves(first, tile_ref, recv_ref, index_ref, pos, rims_ref, force, lines):
    if first:
        me = tile_ref[0]
        before, after = jnp.maximum(me - 1, 0), jnp.minimum(me + 1, TILES - 1)
        rims_ref[0:8, :] = jnp.broadcast_to(recv_ref[before, 2, 7:8, :], (8, LANES)).astype(
            jnp.int32
        )
        rims_ref[8:16, :] = jnp.broadcast_to(recv_ref[after, 2, 6:7, :], (8, LANES)).astype(
            jnp.int32
        )
        count, base = 6, 3
    else:
        count, base = 3, 0
    slot = index_ref[...]
    parts = pick(lambda c, r: recv_ref[r, 1, c : c + 1, :], count, slot >> 7, slot & 127)
    ends = []
    for side in range(2):
        slot = rims_ref[8 * side : 8 * side + 8, :]
        block = 2 * side
        ends.append(
            pick(lambda c, r: recv_ref[r, block, c : c + 1, :], count, slot >> 7, slot & 127)
        )
    live = (
        jnp.where(tile_ref[0] > 0, stokes_coef, 0.0),
        jnp.where(tile_ref[0] < TILES - 1, stokes_coef, 0.0),
    )
    for c in range(3):
        if first:
            pos[c, 0:1, :] = ends[0][c][:1] - 0.5
            pos[c, 1 : ROWS + 1, :] = parts[c] - 0.5
            pos[c, ROWS + 1 : ROWS + 2, :] = ends[1][c][:1] - 0.5
            pos[c, ROWS + 2 :, :] = jnp.zeros((PITCH - ROWS - 2, LANES), F32)
        force[c, 0:1, :] = ends[0][base + c][:1] * live[0]
        force[c, 1 : ROWS + 1, :] = parts[base + c] * stokes_coef
        force[c, ROWS + 1 : ROWS + 2, :] = ends[1][base + c][:1] * live[1]
        force[c, ROWS + 2 :, :] = jnp.zeros((PITCH - ROWS - 2, LANES), F32)

    def plane(k):
        return slice(k * PITCH, (k + 1) * PITCH)

    lines[0, plane(6), :] = jnp.zeros((PITCH, LANES), F32)
    lines[0, plane(7), :] = jnp.zeros((PITCH, LANES), F32)
    lines[1, plane(6), :] = jnp.ones((PITCH, LANES), F32)
    lines[1, plane(7), :] = jnp.zeros((PITCH, LANES), F32)
    for k, ref in enumerate((force, pos)):
        for c in range(3):
            lines[k, plane(c), :], lines[k, plane(3 + c), :] = halves(ref[c])


def body_kernel(
    first, last, tile_ref, got_ref, mate_ref, op_ref, take_ref, mine_ref, info_ref, recv_ref,
    *refs,
):
    z_ref, corr_ref = refs[:2]
    rows, full_ref = refs[-2:]
    side = tile_ref[0] & 1
    for s in range(TILES // 2):
        full_ref[2 * s + side] = got_ref[s]
        full_ref[2 * s + 1 - side] = mate_ref[s]
    full = full_ref[...].reshape(TILES * COLS, LANES)
    z = jnp.dot(op_ref[...], full, preferred_element_type=F32)
    got = jnp.dot(take_ref[...], full, preferred_element_type=F32)
    mine = mine_ref[...]
    lane = lane_iota(FIB)
    corr = jnp.zeros((FIB, LANES), F32)
    for c in range(3):
        value = jnp.sum(got[c * FIB : (c + 1) * FIB] * mine, axis=1, keepdims=True)
        corr = jnp.where(lane == c, value * -kappa_coef, corr)
    corr_ref[...] = corr
    for s in range(TILES):
        rows[0, s : s + 1, :] = recv_ref[s, 1, 6:7, :] if first else recv_ref[s, 0, 3:4, :]
        rows[1, s : s + 1, :] = recv_ref[s, 1, 7:8, :] if first else recv_ref[s, 1, 3:4, :]
    low = lane_iota(TILES) < FNODES
    ra, rb = rows[0], rows[1]
    wa, wb = pltpu.roll(ra, FNODES, 1), pltpu.roll(rb, FNODES, 1)
    for c, value in enumerate(
        (jnp.where(low, ra, wa), jnp.where(low, rb, wb), jnp.where(low, wa, ra))
    ):
        high = value.astype(BF16).astype(F32)
        rows[c] = jnp.where(low, high, value - high)
    column = (sub_iota(COLS) + tile_ref[0] * COLS).astype(F32)
    nucleus = sub_iota(LANES).astype(F32)
    ends = jnp.zeros((COLS, LANES), F32)
    for s in range(TILES):
        node = info_ref[s, 0, 7:8, :]
        left = jnp.zeros((COLS, LANES), F32)
        for c in range(3):
            left = jnp.where(column == node + float(c * BNODES), rows[c, s : s + 1, :], left)
        right = jnp.where(nucleus == info_ref[s, 0, 6:7, :], 1.0, 0.0).astype(BF16)
        ends = ends + lax.dot_general(
            left.astype(BF16), right, (((1,), (1,)), ((), ())), preferred_element_type=F32
        )
    z = z - kappa_coef * ends
    z_ref[...] = z
    if not last:
        for s in range(TILES // 2):
            refs[2][s] = z.astype(BF16)


def assemble(back_ref, inv_ref, prod_ref, corr_ref, q_ref):
    slot = inv_ref[...]
    h0, h1, h2 = pick(lambda c, r: back_ref[r, c : c + 1, :], 3, slot >> 7, slot & 127)
    lane = lane_iota(ROWS)
    low = lane < FNODES
    blank = jnp.zeros((ROWS, LANES), F32)
    first = (
        jnp.where(low, h0, pltpu.roll(h1, FNODES, 1)),
        jnp.where(low, pltpu.roll(h0, FNODES, 1), h1),
    )
    second = (jnp.where(low, h2, blank), jnp.where(low, pltpu.roll(h2, FNODES, 1), blank))
    for half in range(2):
        rows = slice(half * ROWS, (half + 1) * ROWS)
        c0, c1, c2 = (corr_ref[rows, c : c + 1] for c in range(3))
        at0 = jnp.where(lane == 0, c0, jnp.where(lane == FNODES, c1, blank))
        at1 = jnp.where(lane == 0, c2, blank)
        q_ref[rows, :LANES] = prod_ref[rows, :LANES] + first[half] + at0
        q_ref[rows, LANES:] = prod_ref[rows, LANES:] + second[half] + at1


def join_kernel(
    back_ref, inv_ref, prod_ref, corr_ref, index_ref, q_ref, low_ref, sent_ref, table, mix
):
    assemble(back_ref, inv_ref, prod_ref, corr_ref, q_ref)
    low_ref[...] = q_ref[...].astype(BF16)
    for c, part in enumerate(fiber_table(q_ref)):
        table[c] = part
    row, lane = table_place(index_ref[...])
    forces = pick(lambda c, r: table[c, r : r + 1, :], 3, row, lane)
    even, odd = end_rows(q_ref)
    send_out(mix, forces, [[even], [odd], [odd]], sent_ref, 4)


def dots_kernel(back_ref, inv_ref, prod_ref, corr_ref, *refs):
    q, z, (out_ref, last) = refs[:3], refs[3:7], refs[7:]
    assemble(back_ref, inv_ref, prod_ref, corr_ref, last)
    q = list(q) + [last]
    lane = lane_iota(1)
    line = jnp.zeros((1, LANES), F32)
    k = 0
    for i in range(4):
        for j in range(i + 1):
            total = jnp.sum(q[i][...] * q[j][...]) + jnp.sum(z[i][...] * z[j][...])
            line = jnp.where(lane == k, total, line)
            k += 1
    for d in range(ALL):
        out_ref[d] = line


def solve_kernel(gram_ref, *refs):
    q, z, (fiber_ref, body_ref) = refs[:3], refs[3:6], refs[6:]
    line = jnp.sum(gram_ref[...], axis=0)
    lane = lane_iota(1)
    g = {}
    k = 0
    for i in range(4):
        for j in range(i + 1):
            g[i, j] = g[j, i] = jnp.sum(jnp.where(lane == k, line, 0.0), axis=1, keepdims=True)
            k += 1
    n = {}
    for i in range(3):
        for j in range(i + 1):
            n[i, j] = g[i, j] + g[i + 1, j] + g[i, j + 1] + g[i + 1, j + 1]
    t = [g[0, i] + g[0, i + 1] for i in range(3)]
    l00 = jnp.sqrt(n[0, 0])
    l10, l20 = n[1, 0] / l00, n[2, 0] / l00
    l11 = jnp.sqrt(jnp.maximum(n[1, 1] - l10 * l10, n[1, 1] * 1e-7))
    l21 = (n[2, 1] - l20 * l10) / l11
    l22 = jnp.sqrt(jnp.maximum(n[2, 2] - l20 * l20 - l21 * l21, n[2, 2] * 1e-7))
    f0 = t[0] / l00
    f1 = (t[1] - l10 * f0) / l11
    f2 = (t[2] - l20 * f0 - l21 * f1) / l22
    c2 = f2 / l22
    c1 = (f1 - l21 * c2) / l11
    c0 = (f0 - l10 * c1 - l20 * c2) / l00
    fiber_ref[...] = c0 * q[0][...] + c1 * q[1][...] + c2 * q[2][...]
    body = c0 * z[0][...] + c1 * z[1][...] + c2 * z[2][...]
    body_ref[...] = body[:, :NUC]


def exchange(array, axis=TILE):
    return lax.all_to_all(array, axis, split_axis=0, concat_axis=0, tiled=True)


def local(
    rhs_fiber,
    rhs_body,
    fiber_ops,
    body_op,
    positions,
    send_order,
    leaf_order,
    neighbours,
    attach_nucleus,
    attach_node,
):
    tile = lax.axis_index(TILE).astype(jnp.int32).reshape(1)
    load = shape((TILES // 2, COLS, LANES), BF16)
    wanted = (jnp.arange(3, dtype=jnp.int32)[:, None] * BNODES + attach_node[None, :]).reshape(-1)
    take = (wanted[:, None] == jnp.arange(3 * BNODES, dtype=jnp.int32)[None, :]).astype(BF16)
    mine = (attach_nucleus[:, None] == jnp.arange(LANES, dtype=jnp.int32)[None, :]).astype(F32)

    square = shape((ROWS, LANES), jnp.int32)
    spots = shape((3, PITCH, LANES))
    rims = shape((16, LANES), jnp.int32)
    table = pltpu.VMEM((3, ROWS, LANES), F32)
    pairs = (ROWS, 3, LANES, LANES)
    block = pl.BlockSpec((BATCH, 3, LANES, LANES), lambda i: (i, 0, 0, 0))
    padded = pltpu.VMEM((3, PITCH, LANES), F32)
    mix4 = pltpu.VMEM((4 * ROWS, LANES), F32)
    blocks8 = pltpu.VMEM((8 * PITCH, LANES), F32)
    blocks4 = pltpu.VMEM((4 * PITCH, LANES), F32)

    sent, send_index = call(
        prep_kernel, (shape((ROWS, 3, 8, LANES)), square), [VMEM] * 6, [table, blocks8], 2.0
    )(
        positions,
        rhs_fiber,
        send_order,
        leaf_order,
        attach_nucleus.reshape(1, FIB),
        attach_node.reshape(1, FIB),
    )
    leaf_index, inv_leaf, inv_send, body0, payload = call(
        invert_kernel,
        (square, square, square, shape((COLS, LANES)), load),
        [VMEM] * 3,
        (),
        2.0,
    )(leaf_order, send_order, rhs_body.T)

    q, z, low = [rhs_fiber], [body0], rhs_fiber.astype(BF16)
    for j in range(ITERS):
        first, last = j == 0, j + 1 == ITERS
        recv = exchange(sent)
        product = jnp.einsum(
            "fij,fj->fi", fiber_ops, low, preferred_element_type=F32
        )
        if first:
            recv, product, payload, take, mine = lax.optimization_barrier(
                (recv, product, payload, take, mine)
            )
        else:
            recv, product, payload = lax.optimization_barrier((recv, product, payload))
        got = exchange(payload, "chip")
        near = functools.partial(near_kernel, first)
        specs = [SMEM, SMEM] + [VMEM] * 3
        scratch = [
            padded,
            pltpu.VMEM((2, 8 * PITCH, LANES), F32),
            pltpu.VMEM((UNROLL, 3, LANES, LANES), F32),
            pltpu.VMEM((UNROLL, 3, LANES, LANES), BF16),
            pltpu.VMEM((2, 8 * ROWS, LANES), F32),
            mix4,
        ]
        steps = (ROWS // BATCH,)
        result = shape((ROWS, 4, LANES))
        if first:
            info = recv
            out, pos, rim, *kept = call(
                near,
                (result, spots, rims, shape(pairs, BF16), shape(pairs)),
                specs,
                scratch,
                13.0,
                steps,
                (VMEM, VMEM, VMEM, block, block),
            )(tile, neighbours, recv, leaf_index, inv_leaf)
        else:
            out = call(near, result, specs + [VMEM, VMEM, block, block], scratch, 9.0, steps)(
                tile, neighbours, recv, leaf_index, inv_leaf, pos, rim, *kept
            )
        got, out = lax.optimization_barrier((got, out))
        mate = lax.ppermute(got, "core", [(0, 1), (1, 0)])
        back = exchange(out)
        made = [shape((COLS, LANES)), shape((FIB, LANES))]
        if not last:
            made.append(load)
        image, corr, *rest = call(
            functools.partial(body_kernel, first, last),
            tuple(made),
            [SMEM] + [VMEM] * 7,
            [pltpu.VMEM((3, TILES, LANES), F32), pltpu.VMEM((TILES, COLS, LANES), BF16)],
            4.0,
            mib=14,
        )(tile, got, mate, body_op, take, mine, info, recv)
        z.append(image)
        if not last:
            payload = rest[0]
            vector, low, sent = call(
                join_kernel,
                (shape((FIB, ORDER)), shape((FIB, ORDER), BF16), shape((ROWS, 3, 4, LANES))),
                [VMEM] * 5,
                [table, blocks4],
                2.0,
            )(back, inv_send, product, corr, send_index)
            q.append(vector)
    line = call(
        dots_kernel,
        shape((ALL, 1, LANES)),
        [VMEM] * 11,
        [pltpu.VMEM((FIB, ORDER), F32)],
        2.0,
    )(back, inv_send, product, corr, *q, *z)
    gram = exchange(line, AXES)
    sol_fiber, sol_body = call(
        solve_kernel, (shape((FIB, ORDER)), shape((COLS, NUC))), [VMEM] * 7
    )(gram, *q, *z[:3])
    return sol_fiber, sol_body.T


def solution(mesh):
    groups, tiles = mesh.devices.shape
    split = jax.sharding.Mesh(mesh.devices.reshape(groups, tiles // 2, 2), AXES)
    placed = (
        P(AXES, None),
        P("grp", TILE),
        P(AXES, None, None),
        P(TILE, None),
        P(None, AXES),
        P(AXES, None),
        P(AXES, None),
        P(AXES, None),
        P(AXES),
        P(AXES),
    )
    return jax.shard_map(
        local,
        mesh=split,
        in_specs=placed,
        out_specs=(P(AXES, None), P("grp", TILE)),
        check_vma=False,
    )
```

```python
import functools
import math

import jax
import jax.numpy as jnp
from jax import lax
from jax.experimental import pallas as pl
from jax.experimental.pallas import tpu as pltpu
from jax.sharding import PartitionSpec as P

FNODES = 64
BNODES = 1536
ITERS = 3
FIB = 64
NUC = 100
ORDER = 256
COLS = 144
ROWS = 32
LANES = 128
NODES = ROWS * LANES
PITCH = 40
UNROLL = 8
BATCH = 8
TILES = 32
ALL = 128

kappa_coef = 0.5
eps_square = 0.0025
stokes_coef = 1.0 / (16.0 * math.pi)

F32 = jnp.float32
BF16 = jnp.bfloat16
TILE = ("chip", "core")
AXES = ("grp",) + TILE


def shape(dims, dtype=F32):
    return jax.ShapeDtypeStruct(dims, dtype)


VMEM = pl.BlockSpec(memory_space=pltpu.VMEM)
SMEM = pl.BlockSpec(memory_space=pltpu.SMEM)


def call(body, outs, in_specs, scratch=(), micros=1.0, grid=(), out_specs=None, mib=None):
    return pl.pallas_call(
        body,
        out_shape=outs,
        grid=grid,
        in_specs=in_specs,
        out_specs=out_specs or jax.tree.map(lambda _: VMEM, outs),
        scratch_shapes=list(scratch),
        compiler_params=pltpu.CompilerParams(vmem_limit_bytes=mib and mib << 20),
        cost_estimate=pl.CostEstimate(
            flops=0, transcendentals=0, bytes_accessed=int(micros * 3.6e6)
        ),
    )


def lane_iota(rows):
    return lax.broadcasted_iota(jnp.int32, (rows, LANES), 1)


def sub_iota(rows):
    return lax.broadcasted_iota(jnp.int32, (rows, LANES), 0)


def pick(read, count, row, lane):
    size = row.shape
    outs = [jnp.zeros(size, F32)] * count
    for r in range(ROWS):
        hit = row == r
        for c in range(count):
            source = jnp.broadcast_to(read(c, r), size)
            found = jnp.take_along_axis(source, lane, axis=1, mode="promise_in_bounds")
            outs[c] = jnp.where(hit, found, outs[c])
    return outs


def swap_out(mix, parts, out_ref, width):
    for c in range(width):
        mix[c * ROWS : (c + 1) * ROWS, :] = parts[min(c, len(parts) - 1)]
    for d in range(ROWS):
        out_ref[d] = mix[pl.ds(d, width, stride=ROWS), :]


def send_out(mix, parts, extras, out_ref, width):
    for c, part in enumerate(parts):
        mix[c * PITCH : c * PITCH + 1, :] = jnp.zeros((1, LANES), F32)
        mix[c * PITCH + ROWS + 1 : c * PITCH + ROWS + 2, :] = jnp.zeros((1, LANES), F32)
        mix[c * PITCH + 1 : c * PITCH + ROWS + 1, :] = part
    for b, rows in enumerate(extras):
        for k, row in enumerate(rows):
            c = len(parts) + k
            mix[c * PITCH : c * PITCH + PITCH, :] = jnp.broadcast_to(row, (PITCH, LANES))
        for d in range(ROWS):
            out_ref[d, b] = mix[pl.ds(d + b, width, stride=PITCH), :]


def end_rows(q_ref):
    turned = jnp.concatenate([q_ref[:, :LANES], q_ref[:, LANES:]], axis=0).T
    return turned[:1, :], turned[FNODES : FNODES + 1, :]


def fiber_table(q_ref):
    low = lane_iota(ROWS) < FNODES
    a0, a1 = q_ref[:ROWS, :LANES], q_ref[:ROWS, LANES:]
    b0, b1 = q_ref[ROWS:, :LANES], q_ref[ROWS:, LANES:]
    t0 = jnp.where(low, a0, pltpu.roll(b0, FNODES, 1))
    t1 = jnp.where(low, pltpu.roll(a0, FNODES, 1), b0)
    t2 = jnp.where(low, a1, pltpu.roll(b1, FNODES, 1))
    return t0, t1, t2


def table_place(node):
    row = (node >> 6) & 31
    lane = ((node >> 11) << 6) | (node & 63)
    return row, lane


def prep_kernel(
    pos_ref, q_ref, order_ref, leaf_ref, nuc_ref, node_ref, sent_ref, index_ref, table, mix
):
    for r in range(ROWS):
        index_ref[r : r + 1, :] = order_ref[:, r * LANES : (r + 1) * LANES]
    node = index_ref[...]
    spots = pick(
        lambda c, r: pos_ref[c : c + 1, r * LANES : (r + 1) * LANES], 3, node >> 7, node & 127
    )
    for c, part in enumerate(fiber_table(q_ref)):
        table[c] = part
    row, lane = table_place(node)
    forces = pick(lambda c, r: table[c, r : r + 1, :], 3, row, lane)
    twice = [jnp.concatenate([r[...], r[...]], axis=1).astype(F32) for r in (nuc_ref, node_ref)]
    rims = [leaf_ref[:, :LANES].astype(F32), leaf_ref[:, NODES - LANES :].astype(F32)]
    send_out(mix, spots + forces, [twice, list(end_rows(q_ref)), rims], sent_ref, 8)


def invert_kernel(
    leaf_ref, send_ref, body_ref, index_ref, inv_leaf_ref, inv_send_ref, z_ref, load_ref
):
    blank = jnp.zeros((COLS, LANES - NUC), F32)
    z = jnp.concatenate([body_ref[...], blank], axis=1)
    z_ref[...] = z
    for s in range(TILES // 2):
        load_ref[s] = z.astype(BF16)
    slots = lane_iota(64)
    upper = sub_iota(64) >= 32
    spot = sub_iota(64) & 31

    def one(place, row_of, lane_of):
        value = slots + place * LANES
        digit = jnp.where(upper, value & 63, value >> 6).astype(F32)
        left = jnp.where(row_of == spot, digit, 0.0).astype(BF16)
        right = jnp.where(lane_of == sub_iota(LANES), 1.0, 0.0).astype(BF16)
        return lax.dot_general(
            left, right, (((1,), (1,)), ((), ())), preferred_element_type=F32
        )

    leaf_sum = jnp.zeros((64, LANES), F32)
    send_sum = jnp.zeros((64, LANES), F32)
    for r in range(ROWS):
        leaf = leaf_ref[:, r * LANES : (r + 1) * LANES]
        index_ref[r : r + 1, :] = leaf
        leaf_sum = leaf_sum + one(r, leaf >> 7, leaf & 127)
        row, lane = table_place(send_ref[:, r * LANES : (r + 1) * LANES])
        send_sum = send_sum + one(r, row, lane)
    for total, ref in ((leaf_sum, inv_leaf_ref), (send_sum, inv_send_ref)):
        ref[...] = (total[:32] * 64.0 + total[32:]).astype(jnp.int32)


def pair_weights(target, spot, force):
    dx, dy, dz = (target[c] - spot[c] for c in range(3))
    root = lax.rsqrt((dx * dx + eps_square) + (dy * dy + dz * dz))
    cube = root * (root * root)
    along = (dx * force[0] + dy * force[1]) + dz * force[2]
    return root + eps_square * cube, cube, along * cube


def halves(value):
    high = value.astype(BF16).astype(F32)
    return high, value - high


def near_kernel(first, tile_ref, mask_ref, recv_ref, index_ref, inv_ref, *refs):
    if first:
        out_ref, pos, rims_ref, near_ref, cube_ref = refs[:5]
    else:
        pos, rims_ref, near_ref, cube_ref, out_ref = refs[:5]
    force, lines, column, weight, total, mix = refs[5:]
    step = pl.program_id(0)

    @pl.when(step == 0)
    def _():
        gather_leaves(
            first, tile_ref, recv_ref, index_ref, pos, rims_ref, force, lines
        )

    def one_leaf(b, u):
        i = step * BATCH + b
        for c in range(3):
            row = pos[c, pl.ds(i + 1, 1), :]
            column[u, c] = jnp.broadcast_to(row, (LANES, LANES)).T
        sums = [jnp.zeros((8, LANES), F32)] * 2
        for w in range(3):
            spot, push = (
                [jnp.broadcast_to(ref[c, pl.ds(i + w, 1), :], (8, LANES)) for c in range(3)]
                for ref in (pos, force)
            )
            inner = (spot[0] * push[0] + spot[1] * push[1]) + spot[2] * push[2]
            for g in range(LANES // 16):
                rows = slice(16 * g, 16 * g + 16)
                found = []
                for h in (16 * g, 16 * g + 8):
                    target = [column[u, c, h : h + 8, :] for c in range(3)]
                    if first:
                        near, cube, turn = pair_weights(target, spot, push)
                        cube_ref[b, w, h : h + 8, :] = cube
                        found.append((turn, near))
                    else:
                        along = (target[0] * push[0] + target[1] * push[1]) + (
                            target[2] * push[2] - inner
                        )
                        found.append((along * cube_ref[b, w, h : h + 8, :],))
                halves_of = [jnp.concatenate(k, axis=0).astype(BF16) for k in zip(*found)]
                weight[u, w, rows, :] = halves_of[0]
                if first:
                    near_ref[b, w, rows, :] = halves_of[1]
            for k, right in enumerate((near_ref[b, w], weight[u, w])):
                left = lines[k, pl.ds(i + w, 8, stride=PITCH), :].astype(BF16)
                part = lax.dot_general(
                    left, right, (((1,), (1,)), ((), ())), preferred_element_type=F32
                )
                if w != 1:
                    part = part * mask_ref[i, w // 2].astype(F32)
                sums[k] = sums[k] + part
        for k in range(2):
            total[k, pl.ds(8 * i, 8), :] = sums[k]

    def leaves(i, carry):
        for u in range(UNROLL):
            one_leaf(i * UNROLL + u, u)
        return carry

    lax.fori_loop(0, BATCH // UNROLL, leaves, 0)

    @pl.when(step == ROWS // BATCH - 1)
    def _():
        weights = total[1, pl.ds(6, ROWS, stride=8), :]

        def gathered(k, c):
            return total[k, pl.ds(c, ROWS, stride=8), :]

        for c in range(3):
            mix[c * ROWS : (c + 1) * ROWS, :] = (
                (gathered(0, c) + gathered(0, 3 + c))
                + pos[c, 1 : ROWS + 1, :] * weights
                - (gathered(1, c) + gathered(1, 3 + c))
            )
        slot = inv_ref[...]
        parts = pick(
            lambda c, r: mix[c * ROWS + r : c * ROWS + r + 1, :], 3, slot >> 7, slot & 127
        )
        swap_out(mix, parts, out_ref, 4)


def gather_leaves(first, tile_ref, recv_ref, index_ref, pos, rims_ref, force, lines):
    if first:
        me = tile_ref[0]
        before, after = jnp.maximum(me - 1, 0), jnp.minimum(me + 1, TILES - 1)
        rims_ref[0:8, :] = jnp.broadcast_to(recv_ref[before, 2, 7:8, :], (8, LANES)).astype(
            jnp.int32
        )
        rims_ref[8:16, :] = jnp.broadcast_to(recv_ref[after, 2, 6:7, :], (8, LANES)).astype(
            jnp.int32
        )
        count, base = 6, 3
    else:
        count, base = 3, 0
    slot = index_ref[...]
    parts = pick(lambda c, r: recv_ref[r, 1, c : c + 1, :], count, slot >> 7, slot & 127)
    ends = []
    for side in range(2):
        slot = rims_ref[8 * side : 8 * side + 8, :]
        block = 2 * side
        ends.append(
            pick(lambda c, r: recv_ref[r, block, c : c + 1, :], count, slot >> 7, slot & 127)
        )
    live = (
        jnp.where(tile_ref[0] > 0, stokes_coef, 0.0),
        jnp.where(tile_ref[0] < TILES - 1, stokes_coef, 0.0),
    )
    for c in range(3):
        if first:
            pos[c, 0:1, :] = ends[0][c][:1] - 0.5
            pos[c, 1 : ROWS + 1, :] = parts[c] - 0.5
            pos[c, ROWS + 1 : ROWS + 2, :] = ends[1][c][:1] - 0.5
            pos[c, ROWS + 2 :, :] = jnp.zeros((PITCH - ROWS - 2, LANES), F32)
        force[c, 0:1, :] = ends[0][base + c][:1] * live[0]
        force[c, 1 : ROWS + 1, :] = parts[base + c] * stokes_coef
        force[c, ROWS + 1 : ROWS + 2, :] = ends[1][base + c][:1] * live[1]
        force[c, ROWS + 2 :, :] = jnp.zeros((PITCH - ROWS - 2, LANES), F32)

    def plane(k):
        return slice(k * PITCH, (k + 1) * PITCH)

    lines[0, plane(6), :] = jnp.zeros((PITCH, LANES), F32)
    lines[0, plane(7), :] = jnp.zeros((PITCH, LANES), F32)
    lines[1, plane(6), :] = jnp.ones((PITCH, LANES), F32)
    lines[1, plane(7), :] = jnp.zeros((PITCH, LANES), F32)
    for k, ref in enumerate((force, pos)):
        for c in range(3):
            lines[k, plane(c), :], lines[k, plane(3 + c), :] = halves(ref[c])


def body_kernel(
    first, last, tile_ref, got_ref, mate_ref, op_ref, take_ref, mine_ref, info_ref, recv_ref,
    *refs,
):
    z_ref, corr_ref = refs[:2]
    rows, full_ref = refs[-2:]
    side = tile_ref[0] & 1
    for s in range(TILES // 2):
        full_ref[2 * s + side] = got_ref[s]
        full_ref[2 * s + 1 - side] = mate_ref[s]
    full = full_ref[...].reshape(TILES * COLS, LANES)
    z = jnp.dot(op_ref[...], full, preferred_element_type=F32)
    got = jnp.dot(take_ref[...], full, preferred_element_type=F32)
    mine = mine_ref[...]
    lane = lane_iota(FIB)
    corr = jnp.zeros((FIB, LANES), F32)
    for c in range(3):
        value = jnp.sum(got[c * FIB : (c + 1) * FIB] * mine, axis=1, keepdims=True)
        corr = jnp.where(lane == c, value * -kappa_coef, corr)
    corr_ref[...] = corr
    for s in range(TILES):
        rows[0, s : s + 1, :] = recv_ref[s, 1, 6:7, :] if first else recv_ref[s, 0, 3:4, :]
        rows[1, s : s + 1, :] = recv_ref[s, 1, 7:8, :] if first else recv_ref[s, 1, 3:4, :]
    low = lane_iota(TILES) < FNODES
    ra, rb = rows[0], rows[1]
    wa, wb = pltpu.roll(ra, FNODES, 1), pltpu.roll(rb, FNODES, 1)
    for c, value in enumerate(
        (jnp.where(low, ra, wa), jnp.where(low, rb, wb), jnp.where(low, wa, ra))
    ):
        high = value.astype(BF16).astype(F32)
        rows[c] = jnp.where(low, high, value - high)
    column = (sub_iota(COLS) + tile_ref[0] * COLS).astype(F32)
    nucleus = sub_iota(LANES).astype(F32)
    ends = jnp.zeros((COLS, LANES), F32)
    for s in range(TILES):
        node = info_ref[s, 0, 7:8, :]
        left = jnp.zeros((COLS, LANES), F32)
        for c in range(3):
            left = jnp.where(column == node + float(c * BNODES), rows[c, s : s + 1, :], left)
        right = jnp.where(nucleus == info_ref[s, 0, 6:7, :], 1.0, 0.0).astype(BF16)
        ends = ends + lax.dot_general(
            left.astype(BF16), right, (((1,), (1,)), ((), ())), preferred_element_type=F32
        )
    z = z - kappa_coef * ends
    z_ref[...] = z
    if not last:
        for s in range(TILES // 2):
            refs[2][s] = z.astype(BF16)


def assemble(back_ref, inv_ref, prod_ref, corr_ref, q_ref):
    slot = inv_ref[...]
    h0, h1, h2 = pick(lambda c, r: back_ref[r, c : c + 1, :], 3, slot >> 7, slot & 127)
    lane = lane_iota(ROWS)
    low = lane < FNODES
    blank = jnp.zeros((ROWS, LANES), F32)
    first = (
        jnp.where(low, h0, pltpu.roll(h1, FNODES, 1)),
        jnp.where(low, pltpu.roll(h0, FNODES, 1), h1),
    )
    second = (jnp.where(low, h2, blank), jnp.where(low, pltpu.roll(h2, FNODES, 1), blank))
    for half in range(2):
        rows = slice(half * ROWS, (half + 1) * ROWS)
        c0, c1, c2 = (corr_ref[rows, c : c + 1] for c in range(3))
        at0 = jnp.where(lane == 0, c0, jnp.where(lane == FNODES, c1, blank))
        at1 = jnp.where(lane == 0, c2, blank)
        q_ref[rows, :LANES] = prod_ref[rows, :LANES] + first[half] + at0
        q_ref[rows, LANES:] = prod_ref[rows, LANES:] + second[half] + at1


def join_kernel(
    back_ref, inv_ref, prod_ref, corr_ref, index_ref, q_ref, low_ref, sent_ref, table, mix
):
    assemble(back_ref, inv_ref, prod_ref, corr_ref, q_ref)
    low_ref[...] = q_ref[...].astype(BF16)
    for c, part in enumerate(fiber_table(q_ref)):
        table[c] = part
    row, lane = table_place(index_ref[...])
    forces = pick(lambda c, r: table[c, r : r + 1, :], 3, row, lane)
    even, odd = end_rows(q_ref)
    send_out(mix, forces, [[even], [odd], [odd]], sent_ref, 4)


def dots_kernel(back_ref, inv_ref, prod_ref, corr_ref, *refs):
    q, z, (out_ref, last) = refs[:3], refs[3:7], refs[7:]
    assemble(back_ref, inv_ref, prod_ref, corr_ref, last)
    q = list(q) + [last]
    lane = lane_iota(1)
    line = jnp.zeros((1, LANES), F32)
    k = 0
    for i in range(4):
        for j in range(i + 1):
            total = jnp.sum(q[i][...] * q[j][...]) + jnp.sum(z[i][...] * z[j][...])
            line = jnp.where(lane == k, total, line)
            k += 1
    for d in range(ALL):
        out_ref[d] = line


def solve_kernel(gram_ref, *refs):
    q, z, (fiber_ref, body_ref) = refs[:3], refs[3:6], refs[6:]
    line = jnp.sum(gram_ref[...], axis=0)
    lane = lane_iota(1)
    g = {}
    k = 0
    for i in range(4):
        for j in range(i + 1):
            g[i, j] = g[j, i] = jnp.sum(jnp.where(lane == k, line, 0.0), axis=1, keepdims=True)
            k += 1
    n = {}
    for i in range(3):
        for j in range(i + 1):
            n[i, j] = g[i, j] + g[i + 1, j] + g[i, j + 1] + g[i + 1, j + 1]
    t = [g[0, i] + g[0, i + 1] for i in range(3)]
    l00 = jnp.sqrt(n[0, 0])
    l10, l20 = n[1, 0] / l00, n[2, 0] / l00
    l11 = jnp.sqrt(jnp.maximum(n[1, 1] - l10 * l10, n[1, 1] * 1e-7))
    l21 = (n[2, 1] - l20 * l10) / l11
    l22 = jnp.sqrt(jnp.maximum(n[2, 2] - l20 * l20 - l21 * l21, n[2, 2] * 1e-7))
    f0 = t[0] / l00
    f1 = (t[1] - l10 * f0) / l11
    f2 = (t[2] - l20 * f0 - l21 * f1) / l22
    c2 = f2 / l22
    c1 = (f1 - l21 * c2) / l11
    c0 = (f0 - l10 * c1 - l20 * c2) / l00
    fiber_ref[...] = c0 * q[0][...] + c1 * q[1][...] + c2 * q[2][...]
    body = c0 * z[0][...] + c1 * z[1][...] + c2 * z[2][...]
    body_ref[...] = body[:, :NUC]


def exchange(array, axis=TILE):
    return lax.all_to_all(array, axis, split_axis=0, concat_axis=0, tiled=True)


def local(
    rhs_fiber,
    rhs_body,
    fiber_ops,
    body_op,
    positions,
    send_order,
    leaf_order,
    neighbours,
    attach_nucleus,
    attach_node,
):
    tile = lax.axis_index(TILE).astype(jnp.int32).reshape(1)
    load = shape((TILES // 2, COLS, LANES), BF16)
    wanted = (jnp.arange(3, dtype=jnp.int32)[:, None] * BNODES + attach_node[None, :]).reshape(-1)
    take = (wanted[:, None] == jnp.arange(3 * BNODES, dtype=jnp.int32)[None, :]).astype(BF16)
    mine = (attach_nucleus[:, None] == jnp.arange(LANES, dtype=jnp.int32)[None, :]).astype(F32)

    square = shape((ROWS, LANES), jnp.int32)
    spots = shape((3, PITCH, LANES))
    rims = shape((16, LANES), jnp.int32)
    table = pltpu.VMEM((3, ROWS, LANES), F32)
    pairs = (ROWS, 3, LANES, LANES)
    block = pl.BlockSpec((BATCH, 3, LANES, LANES), lambda i: (i, 0, 0, 0))
    padded = pltpu.VMEM((3, PITCH, LANES), F32)
    mix4 = pltpu.VMEM((4 * ROWS, LANES), F32)
    blocks8 = pltpu.VMEM((8 * PITCH, LANES), F32)
    blocks4 = pltpu.VMEM((4 * PITCH, LANES), F32)

    sent, send_index = call(
        prep_kernel, (shape((ROWS, 3, 8, LANES)), square), [VMEM] * 6, [table, blocks8], 2.0
    )(
        positions,
        rhs_fiber,
        send_order,
        leaf_order,
        attach_nucleus.reshape(1, FIB),
        attach_node.reshape(1, FIB),
    )
    leaf_index, inv_leaf, inv_send, body0, payload = call(
        invert_kernel,
        (square, square, square, shape((COLS, LANES)), load),
        [VMEM] * 3,
        (),
        2.0,
    )(leaf_order, send_order, rhs_body.T)

    q, z, low = [rhs_fiber], [body0], rhs_fiber.astype(BF16)
    for j in range(ITERS):
        first, last = j == 0, j + 1 == ITERS
        recv = exchange(sent)
        product = jnp.einsum(
            "fij,fj->fi", fiber_ops, low, preferred_element_type=F32
        )
        if first:
            recv, product, payload, take, mine = lax.optimization_barrier(
                (recv, product, payload, take, mine)
            )
        else:
            recv, product, payload = lax.optimization_barrier((recv, product, payload))
        got = exchange(payload, "chip")
        near = functools.partial(near_kernel, first)
        specs = [SMEM, SMEM] + [VMEM] * 3
        scratch = [
            padded,
            pltpu.VMEM((2, 8 * PITCH, LANES), F32),
            pltpu.VMEM((UNROLL, 3, LANES, LANES), F32),
            pltpu.VMEM((UNROLL, 3, LANES, LANES), BF16),
            pltpu.VMEM((2, 8 * ROWS, LANES), F32),
            mix4,
        ]
        steps = (ROWS // BATCH,)
        result = shape((ROWS, 4, LANES))
        if first:
            info = recv
            out, pos, rim, *kept = call(
                near,
                (result, spots, rims, shape(pairs, BF16), shape(pairs)),
                specs,
                scratch,
                13.0,
                steps,
                (VMEM, VMEM, VMEM, block, block),
            )(tile, neighbours, recv, leaf_index, inv_leaf)
        else:
            out = call(near, result, specs + [VMEM, VMEM, block, block], scratch, 9.0, steps)(
                tile, neighbours, recv, leaf_index, inv_leaf, pos, rim, *kept
            )
        got, out = lax.optimization_barrier((got, out))
        mate = lax.ppermute(got, "core", [(0, 1), (1, 0)])
        back = exchange(out)
        made = [shape((COLS, LANES)), shape((FIB, LANES))]
        if not last:
            made.append(load)
        image, corr, *rest = call(
            functools.partial(body_kernel, first, last),
            tuple(made),
            [SMEM] + [VMEM] * 7,
            [pltpu.VMEM((3, TILES, LANES), F32), pltpu.VMEM((TILES, COLS, LANES), BF16)],
            4.0,
            mib=14,
        )(tile, got, mate, body_op, take, mine, info, recv)
        z.append(image)
        if not last:
            payload = rest[0]
            vector, low, sent = call(
                join_kernel,
                (shape((FIB, ORDER)), shape((FIB, ORDER), BF16), shape((ROWS, 3, 4, LANES))),
                [VMEM] * 5,
                [table, blocks4],
                2.0,
            )(back, inv_send, product, corr, send_index)
            q.append(vector)
    line = call(
        dots_kernel,
        shape((ALL, 1, LANES)),
        [VMEM] * 11,
        [pltpu.VMEM((FIB, ORDER), F32)],
        2.0,
    )(back, inv_send, product, corr, *q, *z)
    gram = exchange(line, AXES)
    sol_fiber, sol_body = call(
        solve_kernel, (shape((FIB, ORDER)), shape((COLS, NUC))), [VMEM] * 7
    )(gram, *q, *z[:3])
    return sol_fiber, sol_body.T


def solution(mesh):
    groups, tiles = mesh.devices.shape
    split = jax.sharding.Mesh(mesh.devices.reshape(groups, tiles // 2, 2), AXES)
    placed = (
        P(AXES, None),
        P("grp", TILE),
        P(AXES, None, None),
        P(TILE, None),
        P(None, AXES),
        P(AXES, None),
        P(AXES, None),
        P(AXES, None),
        P(AXES),
        P(AXES),
    )
    return jax.shard_map(
        local,
        mesh=split,
        in_specs=placed,
        out_specs=(P(AXES, None), P("grp", TILE)),
        check_vma=False,
    )
```
